512 devices in a mesh: ka: 128 (over z_lo, y, x, core), pb: 4 (over z_hi).
Axes of the slice: x: 4, y: 4, z: 16 (z_hi: 4, z_lo: 4; z = z_hi * 4 + z_lo), core: 2. Of those that a mesh axis runs over, the one named last changes fastest.
Arguments:
- coupling: float32 [256, 16, 2, 64, 128], P('ka', 'pb'), may hold values from -6 to 6
- gauge: float32 [256, 64, 128], P('ka'), may hold values from -0.5 to 0.5
- kq_index: int32 [16, 256], P(None, 'ka'), may hold values from 0 to 255, as said below
- fine_coords: int32 [3, 256], replicated, may hold values from 0 to 31
- eig_right: float32 [256, 64, 128], P('ka'), may hold values from -0.5 to 0.5
- eig_left: float32 [256, 16, 64, 128], P('ka', 'pb'), may hold values from -0.5 to 0.5
- energy_k: float32 [256, 64], P('ka'), may hold values from -4 to 4
- energy_kq: float32 [256, 16, 64], P('ka', 'pb'), may hold values from -4 to 4
- occupied: int32 [256, 16, 64], P('ka', 'pb'), may hold values 0 or 1
- frequency: float32 [16, 2], P('pb'), may hold values from 0.02 to 0.12
Outputs:
- self_energy: float32 [256, 64], P('ka')
The draws below stay inside these ranges and needn't reach their ends.
Inputs may be any that keep to these rules, and one draw needn't show every extreme that they name: kq_index[q, k] is the number of the coarse point k displaced by the q-th window point's offset on the periodic 8 x 8 x 4 grid; for each q it is a permutation of the coarse points. Among the offsets are (4, 0, 0) and (0, 0, 3).
All inputs are finite; a program needn't handle non-finite values. No bound on the sum of `occupied` on one device may be relied on, other than what follows from the above.
Results may differ from the reference program's by a relative error of at most 0.0001.
Values sent between devices are 32-bit elements; how exact they have to be, the bound alone decides.
No kernel may reach another device: no remote copies, remote signals or barrier semaphores. Data moves between devices by JAX's collectives and lax.ppermute only.
A program may use at most 64 MiB of HBM per device.

```python
import math
import jax
import jax.numpy as jnp
from jax import lax

W = 64
GX = 8
GY = 8
GZ = 4
FG = 32
NBR = 2
NK = 256
NQ = 16
NF = 256


def draw_kq_index(key, part):
    offset_first = jax.random.randint(jax.random.fold_in(key, 11), (NQ,), 0, GX)
    offset_second = jax.random.randint(jax.random.fold_in(key, 12), (NQ,), 0, GY)
    offset_third = jax.random.randint(jax.random.fold_in(key, 13), (NQ,), 0, GZ)
    offset_first = offset_first.at[0].set(GX // 2).at[1].set(0)
    offset_second = offset_second.at[0].set(0).at[1].set(0)
    offset_third = offset_third.at[0].set(0).at[1].set(GZ - 1)
    order = jax.random.permutation(jax.random.fold_in(key, 14), NQ)
    offset_first = offset_first[order][:, None]
    offset_second = offset_second[order][:, None]
    offset_third = offset_third[order][:, None]
    points = jnp.arange(NK, dtype=jnp.int32)[None, :]
    along_first = (points // (GY * GZ) + offset_first) % GX
    along_second = (points // GZ % GY + offset_second) % GY
    along_third = (points % GZ + offset_third) % GZ
    return ((along_first * GY + along_second) * GZ + along_third).astype(jnp.int32)


def touch_ends(drawn, key, smallest, top_value):
    longest = drawn.shape.index(max(drawn.shape))
    spots = []
    for shift in (0, 1):
        where = [jax.random.randint(jax.random.fold_in(key, axis), (), 0, length) for axis, length in enumerate(drawn.shape)]
        where[longest] = (where[longest] + shift) % drawn.shape[longest]
        spots.append(tuple(where))
    return drawn.at[spots[0]].set(smallest).at[spots[1]].set(top_value)


def steps_of(key, shape, pieces, least, high):
    def one(dim, parts):
        draws = jax.random.uniform(jax.random.fold_in(jax.random.fold_in(key, 6), dim), (parts,), jnp.float32, least / len(pieces), high / len(pieces))
        return jnp.repeat(jnp.exp(draws), shape[dim] // parts).reshape((-1,) + (1,) * (len(shape) - dim - 1))

    level = one(*pieces[0])
    for cut in pieces[1:]:
        level = level * one(*cut)
    return level


def scatter_about(own_key, shape, scale, reach, shards=(), kind=jnp.bfloat16):
    drawn = jax.random.normal(own_key, shape, jnp.float32) * scale
    if len(shards) > 0:
        drawn = steps_of(own_key, shape, shards, -0.22, 0.18) * drawn
    return jnp.clip(drawn, min=-reach, max=reach).astype(kind)


def setup_inputs(seed: int = 0) -> dict:
    seeds = jax.random.split(jax.random.key(seed), 11)
    coupling = scatter_about(seeds[0], (NK, NQ, NBR, W, 2 * W), 1.0, 6.0, ((0, 128), (1, 4)), jnp.float32)
    gauge = scatter_about(seeds[1], (NK, W, 2 * W), (2 * W) ** -0.5, 0.5, ((0, 128),), jnp.float32)
    kq_index = draw_kq_index(jax.random.fold_in(seeds[10], 71), 0)
    fine_coords = touch_ends(jax.random.randint(seeds[3], (3, NF), 0, FG), jax.random.fold_in(seeds[3], 1), 0, FG - 1).astype(jnp.int32)
    eig_right = scatter_about(seeds[4], (NF, W, 2 * W), (2 * W) ** -0.5, 0.5, ((0, 128),), jnp.float32)
    eig_left = scatter_about(seeds[5], (NF, NQ, W, 2 * W), (2 * W) ** -0.5, 0.5, ((0, 128), (1, 4)), jnp.float32)
    energy_k = scatter_about(seeds[6], (NF, W), 1.0, 4.0, ((0, 128),), jnp.float32)
    energy_kq = scatter_about(seeds[7], (NF, NQ, W), 1.0, 4.0, ((0, 128), (1, 4)), jnp.float32)
    occupied = touch_ends((jax.random.randint(seeds[8], (NF, NQ, W), 0, 2) < 1).astype(jnp.int32), jax.random.fold_in(seeds[8], 1), 0, 1)
    frequency = jnp.clip(jnp.exp(math.log(0.12) - 1.7917595 * jax.random.uniform(seeds[9], (NQ, NBR), jnp.float32) ** steps_of(seeds[9], (NQ, NBR), ((0, 4),), -0.2, 0.2)), 0.02, 0.12)
    return dict(coupling=coupling, gauge=gauge, kq_index=kq_index, fine_coords=fine_coords, eig_right=eig_right, eig_left=eig_left, energy_k=energy_k, energy_kq=energy_kq, occupied=occupied, frequency=frequency)


PRECISE = lax.Precision.HIGHEST
BROADEN = 0.1
THERMAL = 0.05


def product(left_matrix, right_matrix):
    return jnp.dot(left_matrix, right_matrix, precision=PRECISE, preferred_element_type=jnp.float32)


def phase_tables(fine_coords):
    points = jnp.arange(NK, dtype=jnp.int32)
    along_first = points // (GY * GZ)
    along_second = (points // GZ) % GY
    along_third = points % GZ
    cell_first = along_first - GX // 2
    cell_second = along_second - GY // 2
    cell_third = along_third - GZ // 2
    coarse_index = (cell_first[:, None] * along_first[None, :] * (GY * GZ) + cell_second[:, None] * along_second[None, :] * (GX * GZ) + cell_third[:, None] * along_third[None, :] * (GX * GY)) % NK
    coarse_angles = coarse_index.astype(jnp.float32) * (2.0 * math.pi / NK)
    fine_index = (fine_coords[0][:, None] * cell_first[None, :] + fine_coords[1][:, None] * cell_second[None, :] + fine_coords[2][:, None] * cell_third[None, :]) % FG
    fine_angles = fine_index.astype(jnp.float32) * (2.0 * math.pi / FG)
    return jnp.cos(coarse_angles) / NK, -jnp.sin(coarse_angles) / NK, jnp.cos(fine_angles), jnp.sin(fine_angles)


def right_block(matrix):
    orbitals = matrix.shape[-2]
    real_part = matrix[..., :orbitals]
    imag_part = matrix[..., orbitals:]
    upper_half = jnp.concatenate([real_part, imag_part], -1)
    lower_half = jnp.concatenate([-imag_part, real_part], -1)
    return jnp.concatenate([upper_half, lower_half], -2)


def apply_left(left_gauge, matrices, pattern):
    orbitals = left_gauge.shape[-2]
    swapped = jnp.concatenate([matrices[..., orbitals:], -matrices[..., :orbitals]], -1)
    first_term = jnp.einsum(pattern, left_gauge[..., :orbitals], matrices, precision=PRECISE)
    return first_term + jnp.einsum(pattern, left_gauge[..., orbitals:], swapped, precision=PRECISE)


def sectioned(cols_real, cols_imag, tables):
    coarse_real, coarse_imag, fine_cos, fine_sin = tables
    space_real = product(coarse_real, cols_real) - product(coarse_imag, cols_imag)
    space_imag = product(coarse_real, cols_imag) + product(coarse_imag, cols_real)
    fine_real_part = product(fine_cos, space_real) - product(fine_sin, space_imag)
    fine_imag_part = product(fine_cos, space_imag) + product(fine_sin, space_real)
    return fine_real_part, fine_imag_part


def self_terms(bloch, energy_k, energy_kq, occupied, frequency):
    orbitals = bloch.shape[-2]
    square = bloch * bloch
    strength = square[..., :orbitals] + square[..., orbitals:]
    phonon = frequency[None, :, :, None, None]
    bose_factor = 1.0 / (jnp.exp(phonon / THERMAL) - 1.0)
    filled = occupied.astype(jnp.float32)[:, :, None, :, None]
    energy_gap = energy_k[:, None, None, None, :] - energy_kq[:, :, None, :, None]
    shifted_up = energy_gap + phonon
    shifted_down = energy_gap - phonon
    kernel = (bose_factor + filled) * shifted_up / (shifted_up * shifted_up + BROADEN * BROADEN)
    kernel = kernel + (bose_factor + 1.0 - filled) * shifted_down / (shifted_down * shifted_down + BROADEN * BROADEN)
    return jnp.sum(strength / (2.0 * phonon) * kernel, axis=(1, 2, 3))


def reference(coupling, gauge, kq_index, fine_coords, eig_right, eig_left, energy_k, energy_kq, occupied, frequency):
    tables = phase_tables(fine_coords)
    gauge_block = right_block(gauge)
    fine_block = right_block(eig_right)
    orbitals = gauge.shape[1]
    branches = coupling.shape[2]
    points_fine = fine_coords.shape[1]

    def one_qpoint(qpoint, running_sum):
        coupled = lax.dynamic_index_in_dim(coupling, qpoint, 1, keepdims=False)
        targets = lax.dynamic_index_in_dim(kq_index, qpoint, 0, keepdims=False)
        partner = jnp.take(gauge, targets, axis=0)
        right_gauge = jnp.einsum('kbjc,kcd->kbjd', coupled, gauge_block, precision=PRECISE)
        wannier = apply_left(partner, right_gauge, 'kjm,kbjc->kbmc')
        columns = wannier.reshape(NK, branches, orbitals, 2, orbitals).transpose(0, 3, 1, 2, 4).reshape(NK, 2, -1)
        fine_real_part, fine_imag_part = sectioned(columns[:, 0], columns[:, 1], tables)
        fine_coupling = jnp.stack([fine_real_part, fine_imag_part], 1).reshape(points_fine, 2, branches, orbitals, orbitals)
        fine_coupling = fine_coupling.transpose(0, 2, 3, 1, 4).reshape(points_fine, branches, orbitals, 2 * orbitals)
        left_fine = lax.dynamic_index_in_dim(eig_left, qpoint, 1, keepdims=False)
        half_way = jnp.einsum('fbjc,fcd->fbjd', fine_coupling, fine_block, precision=PRECISE)
        bloch = apply_left(left_fine, half_way, 'fjm,fbjc->fbmc')
        contrib = self_terms(bloch[:, None], energy_k, lax.dynamic_slice_in_dim(energy_kq, qpoint, 1, 1), lax.dynamic_slice_in_dim(occupied, qpoint, 1, 1), lax.dynamic_slice_in_dim(frequency, qpoint, 1, 0))
        return running_sum + contrib

    summed = lax.fori_loop(0, NQ, one_qpoint, jnp.zeros((points_fine, orbitals), jnp.float32))
    return summed / (NQ * orbitals)
```

```python
import functools
import math

import jax
import jax.numpy as jnp
import numpy as np
from jax import lax
from jax.experimental import pallas as pl
from jax.experimental.pallas import tpu as pltpu
from jax.sharding import Mesh
from jax.sharding import PartitionSpec as P

FG = 32
W = 64
LANES = 128
NK = 256
BROADEN = 0.1
THERMAL = 0.05
KA = ("z", "y", "x", "core")
VMEM = pl.BlockSpec(memory_space=pltpu.VMEM)
SMEM = pl.BlockSpec(memory_space=pltpu.SMEM)
CONTRACT_ROWS = (((0,), (0,)), ((), ()))
PLAIN = (((1,), (0,)), ((), ()))


def halves(value):
    high = value.astype(jnp.bfloat16)
    low = (value - high.astype(jnp.float32)).astype(jnp.bfloat16)
    return high, low


def product(left, right, dims):
    left_high, left_low = left
    right_high, right_low = right
    dot = functools.partial(lax.dot_general, dimension_numbers=dims, preferred_element_type=jnp.float32)
    return dot(left_high, right_high) + (dot(left_high, right_low) + dot(left_low, right_high))


def right_block(matrix):
    real_part = matrix[:, :W]
    imag_part = matrix[:, W:]
    upper = jnp.concatenate([real_part, imag_part], -1)
    lower = jnp.concatenate([-imag_part, real_part], -1)
    return jnp.concatenate([upper, lower], 0)


def signs(first):
    lane = lax.broadcasted_iota(jnp.int32, (1, LANES), 1)
    return jnp.where(lane < W, first, -first)


def apply_left(left, right_pair):
    both = product(halves(left), halves(right_pair), CONTRACT_ROWS)
    sign = signs(1.0)
    return [
        both[:W, at : at + LANES] + sign * pltpu.roll(both[W:, at : at + LANES], W, 1)
        for at in (0, LANES)
    ]


def offsets_of(position, kq, qpoint):
    along_z, along_y, along_x, core = (position[i] for i in range(4))
    first = 2 * along_z + along_y // 2
    second = (along_y % 2) * 4 + along_x
    third = 2 * core
    target = kq[position[4] * 4 + qpoint, 0]
    return (
        (target // 32 - first + 8) % 8,
        (target // 4 % 8 - second + 8) % 8,
        (target % 4 - third + 4) % 4,
    )


def source_of(position, offsets):
    row = (position[1] // 2 + offsets[0]) % 2
    second = ((position[1] % 2) * 4 + position[2] + offsets[1]) % 8
    return (row * 2 + second // 4) * 4 + second % 4


def right_kernel(coupling, gauge, out):
    for k in range(2):
        block = halves(right_block(gauge[k]))
        rows = coupling[k].reshape(-1, LANES)
        result = product(halves(rows), block, PLAIN).reshape(4, 2, W, LANES)
        for q in range(4):
            out[q, 2 * k : 2 * k + 2] = result[q]


def send_kernel(position, kq, gathered, out):
    core = position[3]
    for q in range(4):
        offsets = offsets_of(position, kq, q)
        source = source_of(position, offsets)
        for l in range(2):
            third = (2 * (1 - core) + l + offsets[2]) % 4
            out[q, l] = gathered[source, third % 2]


def keep_kernel(position, kq, gathered, swapped, old, out):
    core = position[3]
    for q in range(4):
        offsets = offsets_of(position, kq, q)
        source = source_of(position, offsets)
        for l in range(2):
            third = (2 * core + l + offsets[2]) % 4
            mine = third // 2 == core

            @pl.when(mine)
            def _(q=q, l=l, third=third, source=source):
                out[q, l] = gathered[source, third % 2]

            @pl.when(jnp.logical_not(mine))
            def _(q=q, l=l):
                out[q, l] = swapped[q, l]


def left_kernel(position, kq, arrived, out):
    offsets = offsets_of(position, kq, position[0])
    carry = (position[1] // 2 + offsets[0]) // 2
    for z in range(4):
        plane = (z + carry) % 4
        for l in range(2):
            gauge = arrived[plane, 4 + l]
            pair = jnp.concatenate([arrived[z, 2 * l], arrived[z, 2 * l + 1]], -1)
            for b, wannier in enumerate(apply_left(gauge, pair)):
                for part in range(2):
                    start = (z * 2 + l) * 4 + part * 2 + b
                    out[pl.ds(start, 32, stride=32), :] = wannier[part * 32 : part * 32 + 32]


def phase_kernel(coords, tables, high, low):
    real, imag = None, None
    for axis in range(3):
        divisions = lax.broadcasted_iota(jnp.int32, (FG, NK), 0)
        onehot = (divisions == coords[axis : axis + 1, :]).astype(jnp.float32)
        factor = [
            lax.dot_general(
                onehot,
                tables[axis, part],
                CONTRACT_ROWS,
                precision=lax.Precision.HIGHEST,
                preferred_element_type=jnp.float32,
            )
            for part in range(2)
        ]
        if real is None:
            real, imag = factor
        else:
            real, imag = (
                real * factor[0] - imag * factor[1],
                real * factor[1] + imag * factor[0],
            )
    for row, part in enumerate((real, imag)):
        part_high, part_low = halves(part)
        high[row * NK : row * NK + NK] = part_high
        low[row * NK : row * NK + NK] = part_low


def fourier_kernel(high, low, columns, out):
    parts = [columns[pl.ds(c, NK, stride=4), :] for c in range(4)]
    result = product((high[...], low[...]), halves(jnp.concatenate(parts, -1)), PLAIN)
    sign = signs(-1.0)
    for c in range(4):
        at = c * LANES
        rolled = pltpu.roll(result[NK:, at : at + LANES], W, 1)
        out[pl.ds(c, NK, stride=4), :] = result[:NK, at : at + LANES] + sign * rolled


def bloch_kernel(frequency, arrived, eig_right, eig_left, energy_k, energy_kq, occupied, out):
    lane = lax.broadcasted_iota(jnp.int32, (1, LANES), 1)
    first = lane < W
    states = jnp.concatenate([energy_kq[...], occupied[...].astype(jnp.float32)], -1).T
    energies = jnp.concatenate([energy_k[0:1], energy_k[1:2]], -1)
    strengths = {}
    for f in range(2):
        rows = [
            arrived[pl.ds(q * 256 + f * 4 + part * 2 + b, 32, stride=8), :]
            for q in range(4)
            for b in range(2)
            for part in range(2)
        ]
        half = product(
            halves(jnp.concatenate(rows, 0)), halves(right_block(eig_right[f])), PLAIN
        )
        for q in range(4):
            at = q * LANES
            pair = jnp.concatenate([half[at : at + W], half[at + W : at + LANES]], -1)
            for b, bloch in enumerate(apply_left(eig_left[f, q], pair)):
                square = bloch * bloch
                strengths[f, q, b] = square + pltpu.roll(square, W, 1)
    total = jnp.zeros((W, LANES), jnp.float32)
    for q in range(4):
        energy_left = jnp.where(first, states[:W, q : q + 1], states[:W, q + 4 : q + 5])
        filled = jnp.where(first, states[W:, q : q + 1], states[W:, q + 4 : q + 5])
        gap = energies - energy_left
        for b in range(2):
            phonon = jnp.full((1, LANES), frequency[q, b], jnp.float32)
            bose = 1.0 / (jnp.exp(phonon / THERMAL) - 1.0)
            up = gap + phonon
            down = gap - phonon
            kernel = (bose + filled) * up / (up * up + BROADEN * BROADEN)
            kernel = kernel + (bose + 1.0 - filled) * down / (down * down + BROADEN * BROADEN)
            strength = jnp.where(first, strengths[0, q, b], strengths[1, q, b])
            total = total + strength / (2.0 * phonon) * kernel
    summed = jnp.sum(total, axis=0, keepdims=True) * (1.0 / 1024.0)
    out[0:1] = summed[:, :W]
    out[1:2] = summed[:, W:]


def phase_tables():
    column = np.arange(NK)
    source, z, l = column // 8, column // 2 % 4, column % 2
    y, x, core = source // 8, source // 2 % 4, source % 2
    coordinates = (2 * z + y // 2, (y % 2) * 4 + x, 2 * core + l)
    tables = np.zeros((3, 2, FG, NK), np.float64)
    for axis, (size, where) in enumerate(zip((8, 8, 4), coordinates)):
        steps = np.arange(FG)[:, None] - (FG // size) * where[None, :]
        for cell in range(-size // 2, size // 2):
            angle = 2.0 * math.pi * ((cell * steps) % FG) / FG
            tables[axis, 0] += np.cos(angle) / size
            tables[axis, 1] += np.sin(angle) / size
    return tables.astype(np.float32)


def call(kernel, shapes, specs, flops, **more):
    return pl.pallas_call(
        kernel,
        out_shape=shapes,
        in_specs=specs,
        cost_estimate=pl.CostEstimate(flops=flops, bytes_accessed=1 << 20, transcendentals=0),
        **more,
    )


def f32(*shape):
    return jax.ShapeDtypeStruct(shape, jnp.float32)


def shards(
    coupling,
    gauge,
    kq_index,
    fine_coords,
    eig_right,
    eig_left,
    energy_k,
    energy_kq,
    occupied,
    frequency,
):
    position = jnp.stack([lax.axis_index(name) for name in (*KA, "pb")])
    to_all = jnp.broadcast_to(gauge[None], (16, 2, W, LANES))
    gathered = lax.all_to_all(to_all, ("y", "x"), 0, 0, tiled=True)
    products = call(right_kernel, f32(4, 6, W, LANES), [VMEM, VMEM], 1 << 27)(coupling, gauge)
    high, low = call(
        phase_kernel,
        [jax.ShapeDtypeStruct((2 * NK, NK), jnp.bfloat16)] * 2,
        [VMEM, VMEM],
        1 << 28,
    )(fine_coords, jnp.asarray(phase_tables()))
    sent = call(send_kernel, f32(4, 2, W, LANES), [SMEM, SMEM, VMEM], 1 << 20)(
        position, kq_index, gathered
    )
    swapped = lax.ppermute(sent, "core", [(0, 1), (1, 0)])
    filled = call(
        keep_kernel,
        f32(4, 6, W, LANES),
        [SMEM, SMEM, VMEM, VMEM, pl.BlockSpec(memory_space=pl.ANY)],
        1 << 20,
        grid=(1,),
        out_specs=pl.BlockSpec((4, 2, W, LANES), lambda i: (0, 2, 0, 0)),
        input_output_aliases={4: 0},
    )(position, kq_index, gathered, swapped, products)
    arrived = lax.all_to_all(filled, "z", 0, 0, tiled=True)
    pieces = call(left_kernel, f32(1024, LANES), [SMEM, SMEM, VMEM], 1 << 27)(
        position, kq_index, arrived
    )
    columns = lax.all_to_all(
        pieces.reshape(32, 32, LANES), ("y", "x", "core"), 0, 0, tiled=True
    ).reshape(1024, LANES)
    fine = call(fourier_kernel, f32(1024, LANES), [VMEM, VMEM, VMEM], 1 << 28)(high, low, columns)
    blocks = lax.all_to_all(fine.reshape(128, 8, LANES), KA, 0, 0, tiled=True)
    terms = call(bloch_kernel, f32(2, W), [SMEM] + [VMEM] * 6, 1 << 27)(
        frequency,
        blocks.reshape(1024, LANES),
        eig_right,
        eig_left,
        energy_k,
        energy_kq.reshape(8, W),
        occupied.reshape(8, W),
    )
    return lax.psum(terms, "pb")


def solution(mesh):
    split = Mesh(mesh.devices.reshape(4, 4, 4, 2, mesh.shape["pb"]), (*KA, "pb"))
    return jax.shard_map(
        shards,
        mesh=split,
        in_specs=(
            P(KA, "pb", None, None, None),
            P(KA, None, None),
            P(None, KA),
            P(),
            P(KA, None, None),
            P(KA, "pb", None, None),
            P(KA, None),
            P(KA, "pb", None),
            P(KA, "pb", None),
            P("pb", None),
        ),
        out_specs=P(KA, None),
        check_vma=False,
    )
```

```python
import functools
import math

import jax
import jax.numpy as jnp
import numpy as np
from jax import lax
from jax.experimental import pallas as pl
from jax.experimental.pallas import tpu as pltpu
from jax.sharding import Mesh
from jax.sharding import PartitionSpec as P

FG = 32
W = 64
LANES = 128
NK = 256
BROADEN = 0.1
THERMAL = 0.05
KA = ("z", "y", "x", "core")
VMEM = pl.BlockSpec(memory_space=pltpu.VMEM)
SMEM = pl.BlockSpec(memory_space=pltpu.SMEM)
CONTRACT_ROWS = (((0,), (0,)), ((), ()))
PLAIN = (((1,), (0,)), ((), ()))


def halves(value):
    high = value.astype(jnp.bfloat16)
    low = (value - high.astype(jnp.float32)).astype(jnp.bfloat16)
    return high, low


def product(left, right, dims):
    left_high, left_low = left
    right_high, right_low = right
    dot = functools.partial(lax.dot_general, dimension_numbers=dims, preferred_element_type=jnp.float32)
    return dot(left_high, right_high) + (dot(left_high, right_low) + dot(left_low, right_high))


def right_block(matrix):
    real_part = matrix[:, :W]
    imag_part = matrix[:, W:]
    upper = jnp.concatenate([real_part, imag_part], -1)
    lower = jnp.concatenate([-imag_part, real_part], -1)
    return jnp.concatenate([upper, lower], 0)


def signs(first):
    lane = lax.broadcasted_iota(jnp.int32, (1, LANES), 1)
    return jnp.where(lane < W, first, -first)


def apply_left(left, right_pair):
    both = product(halves(left), halves(right_pair), CONTRACT_ROWS)
    sign = signs(1.0)
    return [
        both[:W, at : at + LANES] + sign * pltpu.roll(both[W:, at : at + LANES], W, 1)
        for at in (0, LANES)
    ]


def offsets_of(position, kq, qpoint):
    along_z, along_y, along_x, core = (position[i] for i in range(4))
    first = 2 * along_z + along_y // 2
    second = (along_y % 2) * 4 + along_x
    third = 2 * core
    target = kq[position[4] * 4 + qpoint, 0]
    return (
        (target // 32 - first + 8) % 8,
        (target // 4 % 8 - second + 8) % 8,
        (target % 4 - third + 4) % 4,
    )


def source_of(position, offsets):
    row = (position[1] // 2 + offsets[0]) % 2
    second = ((position[1] % 2) * 4 + position[2] + offsets[1]) % 8
    return (row * 2 + second // 4) * 4 + second % 4


def right_kernel(position, coupling, gauge, *outs):
    for k in range(2):
        block = halves(right_block(gauge[k]))
        for shift, out in enumerate(outs):
            rows = coupling[k, (position[0] + shift) % 4].reshape(-1, LANES)
            out[k] = product(halves(rows), block, PLAIN).reshape(2, W, LANES)


def pick_kernel(position, kq, gathered, kept, sent, sems):
    core = position[3]
    copies = []
    for q in range(4):
        offsets = offsets_of(position, kq, q)
        source = source_of(position, offsets)
        for l in range(2):
            for side, out in enumerate((kept, sent)):
                owner = core if side == 0 else 1 - core
                third = (2 * owner + l + offsets[2]) % 4
                copies.append(
                    pltpu.make_async_copy(
                        gathered.at[source, third % 2], out.at[q, l], sems.at[side, q, l]
                    )
                )
                copies[-1].start()
    for copy in copies:
        copy.wait()


def left_kernel(position, kq, exchanged, *products_and_out):
    products, out = products_and_out[:4], products_and_out[4]
    offsets = offsets_of(position, kq, position[0])
    carry = (position[1] // 2 + offsets[0]) // 2
    for shift in range(4):
        plane = (position[0] - shift + 4 + carry) % 4
        for l in range(2):
            gauge = exchanged[plane, l]
            pair = jnp.concatenate([products[shift][l, 0], products[shift][l, 1]], -1)
            for b, wannier in enumerate(apply_left(gauge, pair)):
                for part in range(2):
                    start = (part * 2 + b) * 8 + shift * 2 + l
                    out[pl.ds(start, 32, stride=32), :] = wannier[part * 32 : part * 32 + 32]


def phase_kernel(position, coords, tables, high, low):
    real, imag = None, None
    for axis in range(3):
        divisions = lax.broadcasted_iota(jnp.int32, (FG, NK), 0)
        steps = coords[axis : axis + 1, :]
        if axis == 0:
            steps = (steps + (FG - 8 * position[0])) & (FG - 1)
        onehot = (divisions == steps).astype(jnp.float32)
        factor = [
            lax.dot_general(
                onehot,
                tables[axis, part],
                CONTRACT_ROWS,
                precision=lax.Precision.HIGHEST,
                preferred_element_type=jnp.float32,
            )
            for part in range(2)
        ]
        if real is None:
            real, imag = factor
        else:
            real, imag = (
                real * factor[0] - imag * factor[1],
                real * factor[1] + imag * factor[0],
            )
    for row, part in enumerate((real, imag)):
        part_high, part_low = halves(part)
        high[row * NK : row * NK + NK] = part_high
        low[row * NK : row * NK + NK] = part_low


def fourier_kernel(high, low, columns, out):
    step = pl.program_id(0)
    parts = [columns[:, at : at + 8, :].reshape(NK, LANES) for at in (0, 8)]
    result = product((high[...], low[...]), halves(jnp.concatenate(parts, -1)), PLAIN)
    sign = signs(-1.0)
    for c in range(2):
        at = c * LANES
        rolled = pltpu.roll(result[NK:, at : at + LANES], W, 1)
        value = result[:NK, at : at + LANES] + sign * rolled
        for half in range(2):

            @pl.when(step == half)
            def _(half=half, c=c, value=value):
                out[pl.ds(half * 2 + c, NK, stride=4), :] = value


def bloch_kernel(frequency, arrived, eig_right, eig_left, energy_k, energy_kq, occupied, out):
    lane = lax.broadcasted_iota(jnp.int32, (1, LANES), 1)
    first = lane < W
    states = jnp.concatenate([energy_kq[...], occupied[...].astype(jnp.float32)], -1).T
    energies = jnp.concatenate([energy_k[0:1], energy_k[1:2]], -1)
    strengths = {}
    for f in range(2):
        rows = [
            arrived[pl.ds(q * 256 + f * 4 + part * 2 + b, 32, stride=8), :]
            for q in range(4)
            for b in range(2)
            for part in range(2)
        ]
        half = product(
            halves(jnp.concatenate(rows, 0)), halves(right_block(eig_right[f])), PLAIN
        )
        for q in range(4):
            at = q * LANES
            pair = jnp.concatenate([half[at : at + W], half[at + W : at + LANES]], -1)
            for b, bloch in enumerate(apply_left(eig_left[f, q], pair)):
                square = bloch * bloch
                strengths[f, q, b] = square + pltpu.roll(square, W, 1)
    total = jnp.zeros((W, LANES), jnp.float32)
    for q in range(4):
        energy_left = jnp.where(first, states[:W, q : q + 1], states[:W, q + 4 : q + 5])
        filled = jnp.where(first, states[W:, q : q + 1], states[W:, q + 4 : q + 5])
        gap = energies - energy_left
        for b in range(2):
            phonon = jnp.full((1, LANES), frequency[q, b], jnp.float32)
            bose = 1.0 / (jnp.exp(phonon / THERMAL) - 1.0)
            up = gap + phonon
            down = gap - phonon
            kernel = (bose + filled) * up / (up * up + BROADEN * BROADEN)
            kernel = kernel + (bose + 1.0 - filled) * down / (down * down + BROADEN * BROADEN)
            strength = jnp.where(first, strengths[0, q, b], strengths[1, q, b])
            total = total + strength / (2.0 * phonon) * kernel
    summed = jnp.sum(total, axis=0, keepdims=True) * (1.0 / 1024.0)
    out[0:1] = summed[:, :W]
    out[1:2] = summed[:, W:]


def phase_tables():
    column = np.arange(NK)
    source, z, l = column // 8, column // 2 % 4, column % 2
    y, x, core = source // 8, source // 2 % 4, source % 2
    coordinates = (2 * -z + y // 2, (y % 2) * 4 + x, 2 * core + l)
    tables = np.zeros((3, 2, FG, NK), np.float64)
    for axis, (size, where) in enumerate(zip((8, 8, 4), coordinates)):
        steps = np.arange(FG)[:, None] - (FG // size) * where[None, :]
        for cell in range(-size // 2, size // 2):
            angle = 2.0 * math.pi * ((cell * steps) % FG) / FG
            tables[axis, 0] += np.cos(angle) / size
            tables[axis, 1] += np.sin(angle) / size
    return tables.astype(np.float32)


def call(kernel, shapes, specs, flops, vmem=16, **more):
    return pl.pallas_call(
        kernel,
        out_shape=shapes,
        in_specs=specs,
        cost_estimate=pl.CostEstimate(flops=flops, bytes_accessed=1 << 20, transcendentals=0),
        compiler_params=pltpu.CompilerParams(vmem_limit_bytes=vmem << 20),
        **more,
    )


def f32(*shape):
    return jax.ShapeDtypeStruct(shape, jnp.float32)


def spread(products, shift):
    return lax.ppermute(products, "z", [(z, (z + shift) % 4) for z in range(4)])


def shards(
    coupling,
    gauge,
    kq_index,
    fine_coords,
    eig_right,
    eig_left,
    energy_k,
    energy_kq,
    occupied,
    frequency,
):
    position = jnp.stack([lax.axis_index(name) for name in (*KA, "pb")])
    to_all = jnp.broadcast_to(gauge[None], (16, 2, W, LANES))
    gathered = lax.all_to_all(to_all, ("y", "x"), 0, 0, tiled=True)
    products = call(right_kernel, [f32(2, 2, W, LANES)] * 4, [SMEM, VMEM, VMEM], 1 << 27)(
        position, coupling, gauge
    )
    products = [products[0]] + [
        spread(products[shift], shift) for shift in (1, 2, 3)
    ]
    high, low = call(
        phase_kernel,
        [jax.ShapeDtypeStruct((2 * NK, NK), jnp.bfloat16)] * 2,
        [SMEM, VMEM, VMEM],
        1 << 28,
    )(position, fine_coords, jnp.asarray(phase_tables()))
    kept, sent = call(
        pick_kernel,
        [f32(4, 2, W, LANES)] * 2,
        [SMEM, SMEM, pl.BlockSpec(memory_space=pl.ANY)],
        1 << 20,
        scratch_shapes=[pltpu.SemaphoreType.DMA((2, 4, 2))],
    )(position, kq_index, gathered)
    swapped = lax.ppermute(sent, "core", [(0, 1), (1, 0)])
    own_kq = lax.dynamic_slice_in_dim(kq_index[:, 0], lax.axis_index("pb") * 4, 4)
    thirds = (own_kq[:, None] % 4 + jnp.arange(2)[None, :]) % 4
    mine = thirds // 2 == lax.axis_index("core")
    chosen = jnp.where(mine[:, :, None, None], kept, swapped)
    exchanged = lax.all_to_all(chosen, "z", 0, 0, tiled=True)
    pieces = call(left_kernel, f32(1024, LANES), [SMEM, SMEM] + [VMEM] * 5, 1 << 27)(
        position, kq_index, exchanged, *products
    )
    columns = lax.all_to_all(
        pieces.reshape(32, 32, LANES), ("y", "x", "core"), 0, 0, tiled=True
    )
    fixed = pl.BlockSpec((2 * NK, NK), lambda i: (0, 0))
    fine = call(
        fourier_kernel,
        f32(1024, LANES),
        [fixed, fixed, pl.BlockSpec((32, 16, LANES), lambda i: (0, i, 0))],
        1 << 28,
        grid=(2,),
        out_specs=pl.BlockSpec((1024, LANES), lambda i: (0, 0)),
    )(high, low, columns)
    blocks = lax.all_to_all(fine.reshape(128, 8, LANES), KA, 0, 0, tiled=True)
    terms = call(bloch_kernel, f32(2, W), [SMEM] + [VMEM] * 6, 1 << 27)(
        frequency,
        blocks.reshape(1024, LANES),
        eig_right,
        eig_left,
        energy_k,
        energy_kq.reshape(8, W),
        occupied.reshape(8, W),
    )
    return lax.psum(terms, "pb")


def solution(mesh):
    split = Mesh(mesh.devices.reshape(4, 4, 4, 2, mesh.shape["pb"]), (*KA, "pb"))
    return jax.shard_map(
        shards,
        mesh=split,
        in_specs=(
            P(KA, "pb", None, None, None),
            P(KA, None, None),
            P(None, KA),
            P(),
            P(KA, None, None),
            P(KA, "pb", None, None),
            P(KA, None),
            P(KA, "pb", None),
            P(KA, "pb", None),
            P("pb", None),
        ),
        out_specs=P(KA, None),
        check_vma=False,
    )
```

```python
import functools
import math

import jax
import jax.numpy as jnp
import numpy as np
from jax import lax
from jax.experimental import pallas as pl
from jax.experimental.pallas import tpu as pltpu
from jax.sharding import Mesh
from jax.sharding import PartitionSpec as P

FG = 32
W = 64
LANES = 128
NK = 256
BROADEN = 0.1
THERMAL = 0.05
KA = ("z", "y", "x", "core")
VMEM = pl.BlockSpec(memory_space=pltpu.VMEM)
SMEM = pl.BlockSpec(memory_space=pltpu.SMEM)
CONTRACT_ROWS = (((0,), (0,)), ((), ()))
PLAIN = (((1,), (0,)), ((), ()))


def halves(value):
    high = value.astype(jnp.bfloat16)
    low = (value - high.astype(jnp.float32)).astype(jnp.bfloat16)
    return high, low


def product(left, right, dims):
    left_high, left_low = left
    right_high, right_low = right
    dot = functools.partial(lax.dot_general, dimension_numbers=dims, preferred_element_type=jnp.float32)
    return dot(left_high, right_high) + (dot(left_high, right_low) + dot(left_low, right_high))


def right_block(matrix):
    real_part = matrix[:, :W]
    imag_part = matrix[:, W:]
    upper = jnp.concatenate([real_part, imag_part], -1)
    lower = jnp.concatenate([-imag_part, real_part], -1)
    return jnp.concatenate([upper, lower], 0)


def signs(first):
    lane = lax.broadcasted_iota(jnp.int32, (1, LANES), 1)
    return jnp.where(lane < W, first, -first)


def apply_left(left, right_pair):
    both = product(halves(left), halves(right_pair), CONTRACT_ROWS)
    sign = signs(1.0)
    return [
        both[:W, at : at + LANES] + sign * pltpu.roll(both[W:, at : at + LANES], W, 1)
        for at in (0, LANES)
    ]


def offsets_of(position, kq, qpoint):
    along_z, along_y, along_x, core = (position[i] for i in range(4))
    first = 2 * along_z + (along_y >> 1)
    second = ((along_y & 1) << 2) + along_x
    target = kq[(position[4] << 2) + qpoint, 0]
    return (
        ((target >> 5) - first) & 7,
        ((target >> 2) - second) & 7,
        (target - 2 * core) & 3,
    )


def translation(number):
    along_second, along_first = number % 8, number // 8
    pairs = []
    for y in range(4):
        for x in range(4):
            second = ((y % 2) * 4 + x + along_second) % 8
            first = (y // 2 + along_first) % 2
            pairs.append(((first * 2 + second // 4) * 4 + second % 4, y * 4 + x))
    return pairs


def translated(value, number):
    pairs = translation(number)
    if all(source == target for source, target in pairs):
        return value
    return lax.ppermute(value, ("y", "x"), pairs)


def right_kernel(position, coupling, gauge, *outs):
    for k in range(2):
        block = halves(right_block(gauge[k]))
        for shift, out in enumerate(outs):
            rows = coupling[k, (position[0] + shift) & 3].reshape(-1, LANES)
            out[k] = product(halves(rows), block, PLAIN).reshape(2, W, LANES)


def pack_kernel(position, eig_left, eig_right, energy_k, energy_kq, occupied, *outs):
    for shift, out in enumerate(outs):
        q = (position[0] + shift) & 3
        for f in range(2):
            out[f * W : f * W + W] = eig_left[f, q]
            out[LANES + f * W : LANES + f * W + W] = eig_right[f]
            filled = occupied[f, pl.ds(q, 1), :].astype(jnp.float32)
            row = 2 * LANES + f
            out[row : row + 1] = jnp.concatenate([energy_k[f : f + 1], energy_k[f : f + 1]], -1)
            out[row + 2 : row + 3] = jnp.concatenate([energy_kq[f, pl.ds(q, 1), :], filled], -1)
        out[2 * LANES + 4 :] = jnp.zeros((4, LANES), jnp.float32)


def left_kernel(position, kq, kept, swapped, *products_and_out):
    products, out = products_and_out[:4], products_and_out[4]
    core = position[3]
    offsets = offsets_of(position, kq, position[0])
    carry = ((position[1] >> 1) + offsets[0]) >> 1
    for l in range(2):
        third = (2 * core + l + offsets[2]) & 3
        mine = (third >> 1) == core
        for shift in range(4):
            plane = (position[0] - shift + 4 + carry) & 3
            gauge = jnp.where(mine, kept[plane, third & 1], swapped[plane, third & 1])
            pair = jnp.concatenate([products[shift][l, 0], products[shift][l, 1]], -1)
            for b, wannier in enumerate(apply_left(gauge, pair)):
                for part in range(2):
                    start = (part * 2 + b) * 8 + shift * 2 + l
                    out[pl.ds(start, 32, stride=32), :] = wannier[part * 32 : part * 32 + 32]


def phase_kernel(position, coords, tables, high, low):
    real, imag = None, None
    turned = pltpu.roll(coords[...], (NK - W * position[0]) & (NK - 1), 1)
    for axis in range(3):
        divisions = lax.broadcasted_iota(jnp.int32, (FG, NK), 0)
        steps = turned[axis : axis + 1, :]
        if axis == 0:
            steps = (steps + (FG - 8 * position[0])) & (FG - 1)
        onehot = (divisions == steps).astype(jnp.float32)
        factor = [
            lax.dot_general(
                onehot,
                tables[axis, part],
                CONTRACT_ROWS,
                precision=lax.Precision.HIGHEST,
                preferred_element_type=jnp.float32,
            )
            for part in range(2)
        ]
        if real is None:
            real, imag = factor
        else:
            real, imag = (
                real * factor[0] - imag * factor[1],
                real * factor[1] + imag * factor[0],
            )
    for row, part in enumerate((real, imag)):
        part_high, part_low = halves(part)
        high[row * NK : row * NK + NK] = part_high
        low[row * NK : row * NK + NK] = part_low


def fourier_kernel(high, low, columns, out):
    step = pl.program_id(0)
    parts = [columns[:, at : at + 8, :].reshape(NK, LANES) for at in (0, 8)]
    result = product((high[...], low[...]), halves(jnp.concatenate(parts, -1)), PLAIN)
    sign = signs(-1.0)
    for c in range(2):
        at = c * LANES
        rolled = pltpu.roll(result[NK:, at : at + LANES], W, 1)
        value = result[:NK, at : at + LANES] + sign * rolled
        for half in range(2):

            @pl.when(step == half)
            def _(half=half, c=c, value=value):
                for block in range(8):
                    start = block * 4 + half * 2 + c
                    out[pl.ds(start, 32, stride=32), :] = value[block * 32 : block * 32 + 32]


def bloch_kernel(position, frequency, arrived, *packs_and_out):
    packs, out = packs_and_out[:4], packs_and_out[4]
    lane = lax.broadcasted_iota(jnp.int32, (1, LANES), 1)
    first = lane < W
    phonons = [
        jnp.full((1, LANES), frequency[position[0], b], jnp.float32) for b in range(2)
    ]
    boses = [1.0 / (jnp.exp(phonon / THERMAL) - 1.0) for phonon in phonons]
    for shift, pack in enumerate(packs):
        tail = pack[2 * LANES :]
        energies = jnp.where(first, tail[0:1], tail[1:2])
        states = tail.T
        energy_left = jnp.where(first, states[:W, 2:3], states[:W, 3:4])
        filled = jnp.where(first, states[W:, 2:3], states[W:, 3:4])
        gap = energies - energy_left
        strengths = []
        for f in range(2):
            rows = [
                arrived[pl.ds((-shift % 4 * 2 + f) * 4 + part * 2 + b, 32, stride=32), :]
                for b in range(2)
                for part in range(2)
            ]
            eig_right = pack[LANES + f * W : LANES + f * W + W]
            half = product(
                halves(jnp.concatenate(rows, 0)), halves(right_block(eig_right)), PLAIN
            )
            pair = jnp.concatenate([half[:W], half[W:]], -1)
            blochs = apply_left(pack[f * W : f * W + W], pair)
            squares = [bloch * bloch for bloch in blochs]
            strengths.append([square + pltpu.roll(square, W, 1) for square in squares])
        total = jnp.zeros((W, LANES), jnp.float32)
        for b, (phonon, bose) in enumerate(zip(phonons, boses)):
            up = gap + phonon
            down = gap - phonon
            kernel = (bose + filled) * up / (up * up + BROADEN * BROADEN)
            kernel = kernel + (bose + 1.0 - filled) * down / (down * down + BROADEN * BROADEN)
            strength = jnp.where(first, strengths[0][b], strengths[1][b])
            total = total + strength / (2.0 * phonon) * kernel
        summed = jnp.sum(total, axis=0, keepdims=True) * (1.0 / 1024.0)
        plane = (position[0] - shift + 4) & 3
        for group in range(4):
            out[plane * 4 + group] = summed


def sum_kernel(terms, out):
    summed = jnp.sum(terms[...], axis=0)
    out[0:1] = summed[:, :W]
    out[1:2] = summed[:, W:]


def phase_tables():
    column = np.arange(NK)
    source, z, l = column // 8, column // 2 % 4, column % 2
    y, x, core = source // 8, source // 2 % 4, source % 2
    coordinates = (2 * -z + y // 2, (y % 2) * 4 + x, 2 * core + l)
    tables = np.zeros((3, 2, FG, NK), np.float64)
    for axis, (size, where) in enumerate(zip((8, 8, 4), coordinates)):
        steps = np.arange(FG)[:, None] - (FG // size) * where[None, :]
        for cell in range(-size // 2, size // 2):
            angle = 2.0 * math.pi * ((cell * steps) % FG) / FG
            tables[axis, 0] += np.cos(angle) / size
            tables[axis, 1] += np.sin(angle) / size
    return tables.astype(np.float32)


def call(kernel, shapes, specs, flops, vmem=16, **more):
    return pl.pallas_call(
        kernel,
        out_shape=shapes,
        in_specs=specs,
        cost_estimate=pl.CostEstimate(flops=flops, bytes_accessed=1 << 20, transcendentals=0),
        compiler_params=pltpu.CompilerParams(vmem_limit_bytes=vmem << 20),
        **more,
    )


def f32(*shape):
    return jax.ShapeDtypeStruct(shape, jnp.float32)


def spread(values):
    arrived = [values[0]]
    for shift in (1, 2, 3):
        pairs = [(z, (z + shift) % 4) for z in range(4)]
        arrived.append(lax.ppermute(values[shift], "z", pairs))
    return arrived


def shards(
    coupling,
    gauge,
    kq_index,
    fine_coords,
    eig_right,
    eig_left,
    energy_k,
    energy_kq,
    occupied,
    frequency,
):
    along_z, along_y, along_x, _, pb = (lax.axis_index(name) for name in (*KA, "pb"))
    position = jnp.stack([lax.axis_index(name) for name in (*KA, "pb")])
    planes = lax.all_to_all(jnp.broadcast_to(gauge[None], (4, 2, W, LANES)), "z", 0, 0, tiled=True)
    products = call(right_kernel, [f32(2, 2, W, LANES)] * 4, [SMEM, VMEM, VMEM], 1 << 27)(
        position, coupling, gauge
    )
    products = spread(products)
    packs = call(pack_kernel, [f32(264, LANES)] * 4, [SMEM] + [VMEM] * 5, 1 << 20)(
        position, eig_left, eig_right, energy_k, energy_kq, occupied
    )
    target = kq_index[pb * 4 + along_z, 0]
    number = (((target >> 2) - (along_y * 4 + along_x)) & 7) + (
        (((target >> 5) - (along_y >> 1)) & 1) << 3
    )
    branches = [functools.partial(translated, number=number) for number in range(16)]
    kept = lax.switch(number, branches, planes)
    swapped = lax.ppermute(kept, "core", [(0, 1), (1, 0)])
    pieces = call(left_kernel, f32(1024, LANES), [SMEM, SMEM] + [VMEM] * 6, 1 << 27)(
        position, kq_index, kept, swapped, *products
    )
    columns = lax.all_to_all(pieces.reshape(32, 32, LANES), ("y", "x", "core"), 0, 0, tiled=True)
    packs = spread(packs)
    coords = fine_coords.reshape(3, 4, 32, 2).transpose(0, 1, 3, 2).reshape(3, NK)
    coords = jnp.pad(coords, ((0, 5), (0, 0)))
    high, low = call(
        phase_kernel,
        [jax.ShapeDtypeStruct((2 * NK, NK), jnp.bfloat16)] * 2,
        [SMEM, VMEM, VMEM],
        1 << 28,
    )(position, coords, jnp.asarray(phase_tables()))
    fixed = pl.BlockSpec((2 * NK, NK), lambda i: (0, 0))
    fine = call(
        fourier_kernel,
        f32(1024, LANES),
        [fixed, fixed, pl.BlockSpec((32, 16, LANES), lambda i: (0, i, 0))],
        1 << 28,
        grid=(2,),
        out_specs=pl.BlockSpec((1024, LANES), lambda i: (0, 0)),
    )(high, low, columns)
    blocks = lax.all_to_all(fine.reshape(32, 32, LANES), ("y", "x", "core"), 0, 0, tiled=True)
    terms = call(bloch_kernel, f32(16, 1, LANES), [SMEM, SMEM] + [VMEM] * 5, 1 << 27)(
        position, frequency, blocks.reshape(1024, LANES), *packs
    )
    terms = lax.all_to_all(terms, ("z", "pb"), 0, 0, tiled=True)
    return call(sum_kernel, f32(2, W), [VMEM], 1 << 12)(terms)


def solution(mesh):
    split = Mesh(mesh.devices.reshape(4, 4, 4, 2, mesh.shape["pb"]), (*KA, "pb"))
    return jax.shard_map(
        shards,
        mesh=split,
        in_specs=(
            P(KA, "pb", None, None, None),
            P(KA, None, None),
            P(None, KA),
            P(),
            P(KA, None, None),
            P(KA, "pb", None, None),
            P(KA, None),
            P(KA, "pb", None),
            P(KA, "pb", None),
            P("pb", None),
        ),
        out_specs=P(KA, None),
        check_vma=False,
    )
```

```python
import functools
import math

import jax
import jax.numpy as jnp
import numpy as np
from jax import lax
from jax.experimental import pallas as pl
from jax.experimental.pallas import tpu as pltpu
from jax.sharding import Mesh
from jax.sharding import PartitionSpec as P

FG = 32
W = 64
LANES = 128
NK = 256
BROADEN = 0.1
THERMAL = 0.05
KA = ("z", "y", "x", "core")
VMEM = pl.BlockSpec(memory_space=pltpu.VMEM)
SMEM = pl.BlockSpec(memory_space=pltpu.SMEM)
CONTRACT_ROWS = (((0,), (0,)), ((), ()))
PLAIN = (((1,), (0,)), ((), ()))


def halves(value):
    high = value.astype(jnp.bfloat16)
    low = (value - high.astype(jnp.float32)).astype(jnp.bfloat16)
    return high, low


def product(left, right, dims):
    left_high, left_low = left
    right_high, right_low = right
    dot = functools.partial(lax.dot_general, dimension_numbers=dims, preferred_element_type=jnp.float32)
    return dot(left_high, right_high) + (dot(left_high, right_low) + dot(left_low, right_high))


def right_block(matrix):
    real_part = matrix[:, :W]
    imag_part = matrix[:, W:]
    upper = jnp.concatenate([real_part, imag_part], -1)
    lower = jnp.concatenate([-imag_part, real_part], -1)
    return jnp.concatenate([upper, lower], 0)


def signs(first):
    lane = lax.broadcasted_iota(jnp.int32, (1, LANES), 1)
    return jnp.where(lane < W, first, -first)


def apply_left(left, right_pair):
    both = product(halves(left), halves(right_pair), CONTRACT_ROWS)
    sign = signs(1.0)
    return [
        both[:W, at : at + LANES] + sign * pltpu.roll(both[W:, at : at + LANES], W, 1)
        for at in (0, LANES)
    ]


def offsets_of(position):
    along_z, along_y, along_x, core = (position[i] for i in range(4))
    first = 2 * along_z + (along_y >> 1)
    second = ((along_y & 1) << 2) + along_x
    target = position[4]
    return (
        ((target >> 5) - first) & 7,
        ((target >> 2) - second) & 7,
        (target - 2 * core) & 3,
    )


def translation(number):
    along_second, along_first = number % 8, number // 8
    pairs = []
    for y in range(4):
        for x in range(4):
            second = ((y % 2) * 4 + x + along_second) % 8
            first = (y // 2 + along_first) % 2
            pairs.append(((first * 2 + second // 4) * 4 + second % 4, y * 4 + x))
    return pairs


def translated(value, number):
    pairs = translation(number)
    if all(source == target for source, target in pairs):
        return value
    return lax.ppermute(value, ("y", "x"), pairs)


def right_kernel(coupling, gauge, out):
    for k in range(2):
        block = halves(right_block(gauge[k]))
        rows = coupling[k].reshape(-1, LANES)
        result = product(halves(rows), block, PLAIN).reshape(4, 2, W, LANES)
        for q in range(4):
            out[q, k] = result[q]


def pack_kernel(position, eig_left, eig_right, energy_k, energy_kq, occupied, *outs):
    for shift, out in enumerate(outs):
        q = (position[0] + shift) & 3
        for f in range(2):
            out[f * W : f * W + W] = eig_left[f, q]
            out[LANES + f * W : LANES + f * W + W] = eig_right[f]
            filled = occupied[f, pl.ds(q, 1), :].astype(jnp.float32)
            row = 2 * LANES + f
            out[row : row + 1] = jnp.concatenate([energy_k[f : f + 1], energy_k[f : f + 1]], -1)
            out[row + 2 : row + 3] = jnp.concatenate([energy_kq[f, pl.ds(q, 1), :], filled], -1)
        out[2 * LANES + 4 :] = jnp.zeros((4, LANES), jnp.float32)


def left_kernel(position, kept, swapped, products, out):
    core = position[3]
    offsets = offsets_of(position)
    carry = ((position[1] >> 1) + offsets[0]) >> 1
    for l in range(2):
        third = (2 * core + l + offsets[2]) & 3
        mine = (third >> 1) == core
        for z in range(4):
            plane = (z + carry) & 3
            gauge = jnp.where(mine, kept[plane, third & 1], swapped[plane, third & 1])
            pair = jnp.concatenate([products[z, l, 0], products[z, l, 1]], -1)
            for b, wannier in enumerate(apply_left(gauge, pair)):
                for part in range(2):
                    start = (part * 2 + b) * 8 + z * 2 + l
                    out[pl.ds(start, 32, stride=32), :] = wannier[part * 32 : part * 32 + 32]


def phase_kernel(position, coords, tables, high, low):
    real, imag = None, None
    turned = pltpu.roll(coords[...], (NK - W * position[0]) & (NK - 1), 1)
    for axis in range(3):
        divisions = lax.broadcasted_iota(jnp.int32, (FG, NK), 0)
        steps = turned[axis : axis + 1, :]
        onehot = (divisions == steps).astype(jnp.float32)
        factor = [
            lax.dot_general(
                onehot,
                tables[axis, part],
                CONTRACT_ROWS,
                precision=lax.Precision.HIGHEST,
                preferred_element_type=jnp.float32,
            )
            for part in range(2)
        ]
        if real is None:
            real, imag = factor
        else:
            real, imag = (
                real * factor[0] - imag * factor[1],
                real * factor[1] + imag * factor[0],
            )
    for row, part in enumerate((real, imag)):
        part_high, part_low = halves(part)
        high[row * NK : row * NK + NK] = part_high
        low[row * NK : row * NK + NK] = part_low


def fourier_kernel(high, low, columns, out):
    step = pl.program_id(0)
    parts = [columns[:, at : at + 8, :].reshape(NK, LANES) for at in (0, 8)]
    result = product((high[...], low[...]), halves(jnp.concatenate(parts, -1)), PLAIN)
    sign = signs(-1.0)
    for c in range(2):
        at = c * LANES
        rolled = pltpu.roll(result[NK:, at : at + LANES], W, 1)
        value = result[:NK, at : at + LANES] + sign * rolled
        for half in range(2):

            @pl.when(step == half)
            def _(half=half, c=c, value=value):
                for block in range(8):
                    start = block * 4 + half * 2 + c
                    out[pl.ds(start, 32, stride=32), :] = value[block * 32 : block * 32 + 32]


def bloch_kernel(position, frequency, arrived, *packs_and_out):
    packs, out = packs_and_out[:4], packs_and_out[4]
    lane = lax.broadcasted_iota(jnp.int32, (1, LANES), 1)
    first = lane < W
    phonons = [
        jnp.full((1, LANES), frequency[position[0], b], jnp.float32) for b in range(2)
    ]
    boses = [1.0 / (jnp.exp(phonon / THERMAL) - 1.0) for phonon in phonons]
    for shift, pack in enumerate(packs):
        tail = pack[2 * LANES :]
        energies = jnp.where(first, tail[0:1], tail[1:2])
        states = tail.T
        energy_left = jnp.where(first, states[:W, 2:3], states[:W, 3:4])
        filled = jnp.where(first, states[W:, 2:3], states[W:, 3:4])
        gap = energies - energy_left
        strengths = []
        for f in range(2):
            rows = [
                arrived[pl.ds((-shift % 4 * 2 + f) * 4 + part * 2 + b, 32, stride=32), :]
                for b in range(2)
                for part in range(2)
            ]
            eig_right = pack[LANES + f * W : LANES + f * W + W]
            half = product(
                halves(jnp.concatenate(rows, 0)), halves(right_block(eig_right)), PLAIN
            )
            pair = jnp.concatenate([half[:W], half[W:]], -1)
            blochs = apply_left(pack[f * W : f * W + W], pair)
            squares = [bloch * bloch for bloch in blochs]
            strengths.append([square + pltpu.roll(square, W, 1) for square in squares])
        total = jnp.zeros((W, LANES), jnp.float32)
        for b, (phonon, bose) in enumerate(zip(phonons, boses)):
            up = gap + phonon
            down = gap - phonon
            kernel = (bose + filled) * up / (up * up + BROADEN * BROADEN)
            kernel = kernel + (bose + 1.0 - filled) * down / (down * down + BROADEN * BROADEN)
            strength = jnp.where(first, strengths[0][b], strengths[1][b])
            total = total + strength / (2.0 * phonon) * kernel
        summed = jnp.sum(total, axis=0, keepdims=True) * (1.0 / 1024.0)
        plane = (position[0] - shift + 4) & 3
        for group in range(4):
            out[plane * 4 + group] = summed


def sum_kernel(terms, out):
    summed = jnp.sum(terms[...], axis=0)
    out[0:1] = summed[:, :W]
    out[1:2] = summed[:, W:]


def phase_tables():
    column = np.arange(NK)
    source, z, l = column // 8, column // 2 % 4, column % 2
    y, x, core = source // 8, source // 2 % 4, source % 2
    coordinates = (2 * z + y // 2, (y % 2) * 4 + x, 2 * core + l)
    tables = np.zeros((3, 2, FG, NK), np.float64)
    for axis, (size, where) in enumerate(zip((8, 8, 4), coordinates)):
        steps = np.arange(FG)[:, None] - (FG // size) * where[None, :]
        for cell in range(-size // 2, size // 2):
            angle = 2.0 * math.pi * ((cell * steps) % FG) / FG
            tables[axis, 0] += np.cos(angle) / size
            tables[axis, 1] += np.sin(angle) / size
    return tables.astype(np.float32)


def call(kernel, shapes, specs, flops, vmem=16, **more):
    return pl.pallas_call(
        kernel,
        out_shape=shapes,
        in_specs=specs,
        cost_estimate=pl.CostEstimate(flops=flops, bytes_accessed=1 << 20, transcendentals=0),
        compiler_params=pltpu.CompilerParams(vmem_limit_bytes=vmem << 20),
        **more,
    )


def f32(*shape):
    return jax.ShapeDtypeStruct(shape, jnp.float32)


def spread(value):
    return lax.all_to_all(value, "z", 0, 0, tiled=True)


def shifted(values):
    arrived = [values[0]]
    for shift in (1, 2, 3):
        pairs = [(z, (z + shift) % 4) for z in range(4)]
        arrived.append(lax.ppermute(values[shift], "z", pairs))
    return arrived


def shards(
    coupling,
    gauge,
    kq_index,
    fine_coords,
    eig_right,
    eig_left,
    energy_k,
    energy_kq,
    occupied,
    frequency,
):
    along_z, along_y, along_x, core = (lax.axis_index(name) for name in KA)
    target = kq_index[lax.axis_index("pb") * 4 + along_z, 0]
    position = jnp.stack([along_z, along_y, along_x, core, target])
    planes = spread(jnp.broadcast_to(gauge[None], (4, 2, W, LANES)))
    products = call(right_kernel, f32(4, 2, 2, W, LANES), [VMEM, VMEM], 1 << 27)(coupling, gauge)
    products = spread(products)
    packs = call(pack_kernel, [f32(264, LANES)] * 4, [SMEM] + [VMEM] * 5, 1 << 20)(
        position, eig_left, eig_right, energy_k, energy_kq, occupied
    )
    number = (((target >> 2) - (along_y * 4 + along_x)) & 7) + (
        (((target >> 5) - (along_y >> 1)) & 1) << 3
    )
    branches = [functools.partial(translated, number=number) for number in range(16)]
    kept = lax.switch(number, branches, planes)
    swapped = lax.ppermute(kept, "core", [(0, 1), (1, 0)])
    pieces = call(left_kernel, f32(1024, LANES), [SMEM] + [VMEM] * 3, 1 << 27)(
        position, kept, swapped, products
    )
    columns = lax.all_to_all(pieces.reshape(32, 32, LANES), ("y", "x", "core"), 0, 0, tiled=True)
    packs = shifted(packs)
    coords = fine_coords.reshape(3, 4, 32, 2).transpose(0, 1, 3, 2).reshape(3, NK)
    coords = jnp.pad(coords, ((0, 5), (0, 0)))
    high, low = call(
        phase_kernel,
        [jax.ShapeDtypeStruct((2 * NK, NK), jnp.bfloat16)] * 2,
        [SMEM, VMEM, VMEM],
        1 << 28,
    )(position, coords, jnp.asarray(phase_tables()))
    fixed = pl.BlockSpec((2 * NK, NK), lambda i: (0, 0))
    fine = call(
        fourier_kernel,
        f32(1024, LANES),
        [fixed, fixed, pl.BlockSpec((32, 16, LANES), lambda i: (0, i, 0))],
        1 << 28,
        grid=(2,),
        out_specs=pl.BlockSpec((1024, LANES), lambda i: (0, 0)),
    )(high, low, columns)
    blocks = lax.all_to_all(
        fine.reshape(32, 32, LANES), ("y", "x", "core"), 0, 0, tiled=True
    )
    terms = call(bloch_kernel, f32(16, 1, LANES), [SMEM, SMEM] + [VMEM] * 5, 1 << 27)(
        position, frequency, blocks.reshape(1024, LANES), *packs
    )
    terms = lax.all_to_all(terms, ("z", "pb"), 0, 0, tiled=True)
    return call(sum_kernel, f32(2, W), [VMEM], 1 << 12)(terms)


def solution(mesh):
    split = Mesh(mesh.devices.reshape(4, 4, 4, 2, mesh.shape["pb"]), (*KA, "pb"))
    return jax.shard_map(
        shards,
        mesh=split,
        in_specs=(
            P(KA, "pb", None, None, None),
            P(KA, None, None),
            P(None, KA),
            P(),
            P(KA, None, None),
            P(KA, "pb", None, None),
            P(KA, None),
            P(KA, "pb", None),
            P(KA, "pb", None),
            P("pb", None),
        ),
        out_specs=P(KA, None),
        check_vma=False,
    )
```

```python
import functools
import math

import jax
import jax.numpy as jnp
import numpy as np
from jax import lax
from jax.experimental import pallas as pl
from jax.experimental.pallas import tpu as pltpu
from jax.sharding import Mesh
from jax.sharding import PartitionSpec as P

FG = 32
W = 64
LANES = 128
NK = 256
BROADEN = 0.1
THERMAL = 0.05
KA = ("z", "y", "x", "core")
VMEM = pl.BlockSpec(memory_space=pltpu.VMEM)
SMEM = pl.BlockSpec(memory_space=pltpu.SMEM)
CONTRACT_ROWS = (((0,), (0,)), ((), ()))
PLAIN = (((1,), (0,)), ((), ()))


def halves(value):
    high = value.astype(jnp.bfloat16)
    low = (value - high.astype(jnp.float32)).astype(jnp.bfloat16)
    return high, low


def product(left, right, dims):
    left_high, left_low = left
    right_high, right_low = right
    dot = functools.partial(lax.dot_general, dimension_numbers=dims, preferred_element_type=jnp.float32)
    return dot(left_high, right_high) + (dot(left_high, right_low) + dot(left_low, right_high))


def right_block(matrix):
    real_part = matrix[:, :W]
    imag_part = matrix[:, W:]
    upper = jnp.concatenate([real_part, imag_part], -1)
    lower = jnp.concatenate([-imag_part, real_part], -1)
    return jnp.concatenate([upper, lower], 0)


def signs(first):
    lane = lax.broadcasted_iota(jnp.int32, (1, LANES), 1)
    return jnp.where(lane < W, first, -first)


def apply_left(left, right_pair):
    both = product(halves(left), halves(right_pair), CONTRACT_ROWS)
    sign = signs(1.0)
    return [
        both[:W, at : at + LANES] + sign * pltpu.roll(both[W:, at : at + LANES], W, 1)
        for at in (0, LANES)
    ]


def translation(number):
    along_second, along_first = number % 8, number // 8
    pairs = []
    for y in range(4):
        for x in range(4):
            second = ((y % 2) * 4 + x + along_second) % 8
            first = (y // 2 + along_first) % 2
            pairs.append(((first * 2 + second // 4) * 4 + second % 4, y * 4 + x))
    return pairs


def translated(value, number):
    pairs = translation(number)
    if all(source == target for source, target in pairs):
        return value
    return lax.ppermute(value, ("y", "x"), pairs)


def right_kernel(coupling, gauge, out):
    for k in range(2):
        block = halves(right_block(gauge[k]))
        rows = coupling[k].reshape(-1, LANES)
        result = product(halves(rows), block, PLAIN).reshape(4, 2, W, LANES)
        for q in range(4):
            out[q, k] = result[q]


def pack_kernel(position, _, eig_left, eig_right, energy_k, energy_kq, occupied, *outs):
    for shift, out in enumerate(outs):
        q = (position[0] + shift) & 3
        for f in range(2):
            out[f * W : f * W + W] = eig_left[f, q]
            out[LANES + f * W : LANES + f * W + W] = eig_right[f]
            filled = occupied[f, pl.ds(q, 1), :].astype(jnp.float32)
            row = 2 * LANES + f
            out[row : row + 1] = jnp.concatenate([energy_k[f : f + 1], energy_k[f : f + 1]], -1)
            out[row + 2 : row + 3] = jnp.concatenate([energy_kq[f, pl.ds(q, 1), :], filled], -1)
        out[2 * LANES + 4 :] = jnp.zeros((4, LANES), jnp.float32)


def align_kernel(position, kq, own, other, out):
    core = position[3]
    for q in range(4):
        target = kq[(position[4] << 2) + q, 0]
        for l in range(2):
            third = (target + l) & 3
            mine = (third >> 1) == core
            out[q, l] = jnp.where(mine, own[third & 1], other[third & 1])


def left_kernel(position, number, moved, products, out):
    carry = ((position[1] >> 1) + number[1]) >> 1
    for z in range(4):
        plane = (z + carry) & 3
        for l in range(2):
            pair = jnp.concatenate([products[z, l, 0], products[z, l, 1]], -1)
            for b, wannier in enumerate(apply_left(moved[plane, l], pair)):
                for part in range(2):
                    start = (part * 2 + b) * 8 + z * 2 + l
                    out[pl.ds(start, 32, stride=32), :] = wannier[part * 32 : part * 32 + 32]


def phase_kernel(position, coords, tables, high, low):
    real, imag = None, None
    turned = pltpu.roll(coords[...], (NK - W * position[0]) & (NK - 1), 1)
    for axis in range(3):
        divisions = lax.broadcasted_iota(jnp.int32, (FG, NK), 0)
        steps = turned[axis : axis + 1, :]
        onehot = (divisions == steps).astype(jnp.float32)
        factor = [
            lax.dot_general(
                onehot,
                tables[axis, part],
                CONTRACT_ROWS,
                precision=lax.Precision.HIGHEST,
                preferred_element_type=jnp.float32,
            )
            for part in range(2)
        ]
        if real is None:
            real, imag = factor
        else:
            real, imag = (
                real * factor[0] - imag * factor[1],
                real * factor[1] + imag * factor[0],
            )
    for row, part in enumerate((real, imag)):
        part_high, part_low = halves(part)
        high[row * NK : row * NK + NK] = part_high
        low[row * NK : row * NK + NK] = part_low


def fourier_kernel(high, low, columns, out):
    step = pl.program_id(0)
    parts = [columns[:, at : at + 8, :].reshape(NK, LANES) for at in (0, 8)]
    result = product((high[...], low[...]), halves(jnp.concatenate(parts, -1)), PLAIN)
    sign = signs(-1.0)
    for c in range(2):
        at = c * LANES
        rolled = pltpu.roll(result[NK:, at : at + LANES], W, 1)
        value = result[:NK, at : at + LANES] + sign * rolled
        for half in range(2):

            @pl.when(step == half)
            def _(half=half, c=c, value=value):
                for block in range(8):
                    start = block * 4 + half * 2 + c
                    out[pl.ds(start, 32, stride=32), :] = value[block * 32 : block * 32 + 32]


def bloch_kernel(position, frequency, arrived, *packs_and_out):
    packs, out = packs_and_out[:4], packs_and_out[4]
    lane = lax.broadcasted_iota(jnp.int32, (1, LANES), 1)
    first = lane < W
    phonons = [
        jnp.full((1, LANES), frequency[position[0], b], jnp.float32) for b in range(2)
    ]
    boses = [1.0 / (jnp.exp(phonon / THERMAL) - 1.0) for phonon in phonons]
    for shift, pack in enumerate(packs):
        tail = pack[2 * LANES :]
        energies = jnp.where(first, tail[0:1], tail[1:2])
        states = tail.T
        energy_left = jnp.where(first, states[:W, 2:3], states[:W, 3:4])
        filled = jnp.where(first, states[W:, 2:3], states[W:, 3:4])
        gap = energies - energy_left
        strengths = []
        for f in range(2):
            rows = [
                arrived[pl.ds((-shift % 4 * 2 + f) * 4 + part * 2 + b, 32, stride=32), :]
                for b in range(2)
                for part in range(2)
            ]
            eig_right = pack[LANES + f * W : LANES + f * W + W]
            half = product(
                halves(jnp.concatenate(rows, 0)), halves(right_block(eig_right)), PLAIN
            )
            pair = jnp.concatenate([half[:W], half[W:]], -1)
            blochs = apply_left(pack[f * W : f * W + W], pair)
            squares = [bloch * bloch for bloch in blochs]
            strengths.append([square + pltpu.roll(square, W, 1) for square in squares])
        total = jnp.zeros((W, LANES), jnp.float32)
        for b, (phonon, bose) in enumerate(zip(phonons, boses)):
            up = gap + phonon
            down = gap - phonon
            kernel = (bose + filled) * up / (up * up + BROADEN * BROADEN)
            kernel = kernel + (bose + 1.0 - filled) * down / (down * down + BROADEN * BROADEN)
            strength = jnp.where(first, strengths[0][b], strengths[1][b])
            total = total + strength / (2.0 * phonon) * kernel
        summed = jnp.sum(total, axis=0, keepdims=True) * (1.0 / 1024.0)
        plane = (position[0] - shift + 4) & 3
        for group in range(4):
            out[group * 4 + plane] = summed


def sum_kernel(terms, out):
    summed = jnp.sum(terms[...], axis=0)
    out[0:1] = summed[:, :W]
    out[1:2] = summed[:, W:]


def phase_tables():
    column = np.arange(NK)
    source, z, l = column // 8, column // 2 % 4, column % 2
    y, x, core = source // 8, source // 2 % 4, source % 2
    coordinates = (2 * z + y // 2, (y % 2) * 4 + x, 2 * core + l)
    tables = np.zeros((3, 2, FG, NK), np.float64)
    for axis, (size, where) in enumerate(zip((8, 8, 4), coordinates)):
        steps = np.arange(FG)[:, None] - (FG // size) * where[None, :]
        for cell in range(-size // 2, size // 2):
            angle = 2.0 * math.pi * ((cell * steps) % FG) / FG
            tables[axis, 0] += np.cos(angle) / size
            tables[axis, 1] += np.sin(angle) / size
    return tables.astype(np.float32)


def call(kernel, shapes, specs, flops, vmem=16, **more):
    return pl.pallas_call(
        kernel,
        out_shape=shapes,
        in_specs=specs,
        cost_estimate=pl.CostEstimate(flops=flops, bytes_accessed=1 << 20, transcendentals=0),
        compiler_params=pltpu.CompilerParams(vmem_limit_bytes=vmem << 20),
        **more,
    )


def f32(*shape):
    return jax.ShapeDtypeStruct(shape, jnp.float32)


def spread(value):
    return lax.all_to_all(value, "z", 0, 0, tiled=True)


def shifted(values):
    arrived = [values[0]]
    for shift in (1, 2, 3):
        pairs = [(z, (z + shift) % 4) for z in range(4)]
        arrived.append(lax.ppermute(values[shift], "z", pairs))
    return arrived


def shards(
    coupling,
    gauge,
    kq_index,
    fine_coords,
    eig_right,
    eig_left,
    energy_k,
    energy_kq,
    occupied,
    frequency,
):
    along_z, along_y, along_x, core, pb = (lax.axis_index(name) for name in (*KA, "pb"))
    position = jnp.stack([along_z, along_y, along_x, core, pb])
    other = lax.ppermute(gauge, "core", [(0, 1), (1, 0)])
    aligned = call(align_kernel, f32(4, 2, W, LANES), [SMEM, SMEM, VMEM, VMEM], 1 << 20)(
        position, kq_index, gauge, other
    )
    planes = spread(aligned)
    products = call(right_kernel, f32(4, 2, 2, W, LANES), [VMEM, VMEM], 1 << 27)(coupling, gauge)
    products = spread(products)
    target = kq_index[pb * 4 + along_z, 0]
    along_first = ((target >> 5) - 2 * along_z - (along_y >> 1)) & 7
    along_second = ((target >> 2) - (along_y * 4 + along_x)) & 7
    number = along_second + ((along_first & 1) << 3)
    branches = [functools.partial(translated, number=number) for number in range(16)]
    numbers = jnp.stack([number, along_first])
    packs = call(pack_kernel, [f32(264, LANES)] * 4, [SMEM, SMEM] + [VMEM] * 5, 1 << 20)(
        position, numbers, eig_left, eig_right, energy_k, energy_kq, occupied
    )
    moved = lax.switch(number, branches, planes)
    pieces = call(left_kernel, f32(1024, LANES), [SMEM, SMEM] + [VMEM] * 2, 1 << 27)(
        position, numbers, moved, products
    )
    columns = lax.all_to_all(pieces.reshape(32, 32, LANES), ("y", "x", "core"), 0, 0, tiled=True)
    packs = shifted(packs)
    coords = fine_coords.reshape(3, 4, 32, 2).transpose(0, 1, 3, 2).reshape(3, NK)
    coords = jnp.pad(coords, ((0, 5), (0, 0)))
    high, low = call(
        phase_kernel,
        [jax.ShapeDtypeStruct((2 * NK, NK), jnp.bfloat16)] * 2,
        [SMEM, VMEM, VMEM],
        1 << 28,
    )(position, coords, jnp.asarray(phase_tables()))
    fixed = pl.BlockSpec((2 * NK, NK), lambda i: (0, 0))
    fine = call(
        fourier_kernel,
        f32(1024, LANES),
        [fixed, fixed, pl.BlockSpec((32, 16, LANES), lambda i: (0, i, 0))],
        1 << 28,
        grid=(2,),
        out_specs=pl.BlockSpec((1024, LANES), lambda i: (0, 0)),
    )(high, low, columns)
    blocks = lax.all_to_all(
        fine.reshape(32, 32, LANES), ("y", "x", "core"), 0, 0, tiled=True
    )
    terms = call(bloch_kernel, f32(16, 1, LANES), [SMEM, SMEM] + [VMEM] * 5, 1 << 27)(
        position, frequency, blocks.reshape(1024, LANES), *packs
    )
    terms = lax.all_to_all(terms, ("pb", "z"), 0, 0, tiled=True)
    return call(sum_kernel, f32(2, W), [VMEM], 1 << 12)(terms)


def solution(mesh):
    split = Mesh(mesh.devices.reshape(4, 4, 4, 2, mesh.shape["pb"]), (*KA, "pb"))
    return jax.shard_map(
        shards,
        mesh=split,
        in_specs=(
            P(KA, "pb", None, None, None),
            P(KA, None, None),
            P(None, KA),
            P(),
            P(KA, None, None),
            P(KA, "pb", None, None),
            P(KA, None),
            P(KA, "pb", None),
            P(KA, "pb", None),
            P("pb", None),
        ),
        out_specs=P(KA, None),
        check_vma=False,
    )
```

```python
import functools
import math

import jax
import jax.numpy as jnp
import numpy as np
from jax import lax
from jax.experimental import pallas as pl
from jax.experimental.pallas import tpu as pltpu
from jax.sharding import Mesh
from jax.sharding import PartitionSpec as P

FG = 32
W = 64
LANES = 128
NK = 256
BROADEN = 0.1
THERMAL = 0.05
KA = ("z", "y", "x", "core")
VMEM = pl.BlockSpec(memory_space=pltpu.VMEM)
SMEM = pl.BlockSpec(memory_space=pltpu.SMEM)


def halves(value):
    high = value.astype(jnp.bfloat16)
    low = (value - high.astype(jnp.float32)).astype(jnp.bfloat16)
    return high, low


def product(left, right, axes):
    left_high, left_low = left
    right_high, right_low = right
    return lax.dot_general(
        jnp.concatenate([left_high, left_high, left_low], axes[0]),
        jnp.concatenate([right_high, right_low, right_high], axes[1]),
        (((axes[0],), (axes[1],)), ((), ())),
        preferred_element_type=jnp.float32,
    )


def right_block(matrix):
    turned = signs(-1.0) * pltpu.roll(matrix, W, 1)
    high, low = halves(matrix)
    turned_high, turned_low = halves(turned)
    return jnp.concatenate([high, turned_high], 0), jnp.concatenate([low, turned_low], 0)


def signs(first):
    lane = lax.broadcasted_iota(jnp.int32, (1, LANES), 1)
    return jnp.where(lane < W, first, -first)


def apply_left(left, right_pair):
    both = product(halves(left), halves(right_pair), (0, 0))
    sign = signs(1.0)
    return [
        both[:W, at : at + LANES] + sign * pltpu.roll(both[W:, at : at + LANES], W, 1)
        for at in (0, LANES)
    ]


def translation(number):
    along_second, along_first = number % 8, number // 8
    pairs = []
    for y in range(4):
        for x in range(4):
            second = ((y % 2) * 4 + x + along_second) % 8
            first = (y // 2 + along_first) % 2
            pairs.append(((first * 2 + second // 4) * 4 + second % 4, y * 4 + x))
    return pairs


def translated(value, number):
    pairs = translation(number)
    if all(source == target for source, target in pairs):
        return value
    return lax.ppermute(value, ("y", "x"), pairs)


def right_kernel(coupling, gauge, out):
    for k in range(2):
        block = right_block(gauge[k])
        rows = coupling[k].reshape(-1, LANES)
        result = product(halves(rows), block, (1, 0)).reshape(4, 2, W, LANES)
        for q in range(4):
            out[q, k] = result[q]


def pack_kernel(position, eig_left, eig_right, energy_k, energy_kq, occupied, *outs):
    for shift, out in enumerate(outs):
        q = (position[0] + shift) & 3
        for f in range(2):
            out[f * W : f * W + W] = eig_left[f, q]
            out[LANES + f * W : LANES + f * W + W] = eig_right[f]
            filled = occupied[f, pl.ds(q, 1), :].astype(jnp.float32)
            row = 2 * LANES + f
            out[row : row + 1] = jnp.concatenate([energy_k[f : f + 1], energy_k[f : f + 1]], -1)
            out[row + 2 : row + 3] = jnp.concatenate([energy_kq[f, pl.ds(q, 1), :], filled], -1)
        out[2 * LANES + 4 :] = jnp.zeros((4, LANES), jnp.float32)


def left_kernel(position, kept, swapped, products, out):
    core, target = position[3], position[4]
    first = (target >> 5) - 2 * position[0] - (position[1] >> 1)
    carry = ((position[1] >> 1) + (first & 7)) >> 1
    wanniers = []
    for l in range(2):
        third = (target + l) & 3
        mine = (third >> 1) == core
        for z in range(4):
            plane = (z + carry) & 3
            gauge = jnp.where(mine, kept[plane, third & 1], swapped[plane, third & 1])
            pair = jnp.concatenate([products[z, l, 0], products[z, l, 1]], -1)
            wanniers.append((l, z, apply_left(gauge, pair)))
    for l, z, both in wanniers:
        for b, wannier in enumerate(both):
            for part in range(2):
                start = (part * 2 + b) * 8 + z * 2 + l
                out[pl.ds(start, 32, stride=32), :] = wannier[part * 32 : part * 32 + 32]


def phase_kernel(coords, tables, high, low):
    real, imag = None, None
    divisions = lax.broadcasted_iota(jnp.int32, (FG, NK), 0)
    for axis in range(3):
        onehot = (divisions == coords[axis : axis + 1, :]).astype(jnp.float32)
        onehot = onehot.astype(jnp.bfloat16)
        factor = lax.dot_general(
            jnp.concatenate([onehot] * 3, 0),
            tables[axis],
            (((0,), (0,)), ((), ())),
            preferred_element_type=jnp.float32,
        )
        factor = factor[:, :NK], factor[:, NK:]
        if real is None:
            real, imag = factor
        else:
            real, imag = (
                real * factor[0] - imag * factor[1],
                real * factor[1] + imag * factor[0],
            )
    for row, part in enumerate((real, imag)):
        part_high, part_low = halves(part)
        high[row * NK : row * NK + NK] = part_high
        low[row * NK : row * NK + NK] = part_low


def fourier_kernel(high, low, columns, out):
    parts = [columns[:, at : at + 8, :].reshape(NK, LANES) for at in (0, 8)]
    result = product((high[...], low[...]), halves(jnp.concatenate(parts, -1)), (1, 0))
    sign = signs(-1.0)
    for c in range(2):
        at = c * LANES
        rolled = pltpu.roll(result[NK:, at : at + LANES], W, 1)
        value = result[:NK, at : at + LANES] + sign * rolled
        out[:, c] = value.reshape(32, 8, LANES)


def bloch_kernel(position, frequency, arrived, *packs_and_out):
    packs, out = packs_and_out[:4], packs_and_out[4]
    lane = lax.broadcasted_iota(jnp.int32, (1, LANES), 1)
    first = lane < W
    phonons = [
        jnp.full((1, LANES), frequency[position[0], b], jnp.float32) for b in range(2)
    ]
    boses = [1.0 / (jnp.exp(phonon / THERMAL) - 1.0) for phonon in phonons]
    scales = [1.0 / (2.0 * phonon) for phonon in phonons]
    pairs = []
    for shift, pack in enumerate(packs):
        plane = (position[0] - shift + 4) & 3
        for f in range(2):
            rows = [
                arrived[pl.ds((part * 2 + b) * 8 + plane * 2 + f, 32, stride=32), :]
                for b in range(2)
                for part in range(2)
            ]
            eig_right = pack[LANES + f * W : LANES + f * W + W]
            half = product(halves(jnp.concatenate(rows, 0)), right_block(eig_right), (1, 0))
            pairs.append(jnp.concatenate([half[:W], half[W:]], -1))
    squares = []
    for shift, pack in enumerate(packs):
        for f in range(2):
            blochs = apply_left(pack[f * W : f * W + W], pairs[shift * 2 + f])
            squares.append([bloch * bloch for bloch in blochs])
    for shift, pack in enumerate(packs):
        tail = pack[2 * LANES :]
        energies = jnp.where(first, tail[0:1], tail[1:2])
        states = tail.T
        energy_left = jnp.where(first, states[:W, 2:3], states[:W, 3:4])
        filled = jnp.where(first, states[W:, 2:3], states[W:, 3:4])
        gap = energies - energy_left
        total = jnp.zeros((W, LANES), jnp.float32)
        for b, (phonon, bose) in enumerate(zip(phonons, boses)):
            up = gap + phonon
            down = gap - phonon
            up_square = up * up + BROADEN * BROADEN
            down_square = down * down + BROADEN * BROADEN
            terms = (bose + filled) * up * down_square + (bose + 1.0 - filled) * down * up_square
            one, two = squares[shift * 2][b], squares[shift * 2 + 1][b]
            strength = jnp.where(first, one, two) + pltpu.roll(jnp.where(first, two, one), W, 1)
            total = total + strength * scales[b] * terms / (up_square * down_square)
        summed = jnp.sum(total, axis=0, keepdims=True) * (1.0 / 1024.0)
        plane = (position[0] - shift + 4) & 3
        for group in range(4):
            out[plane * 4 + group] = summed


def sum_kernel(terms, out):
    summed = jnp.sum(terms[...], axis=0)
    out[0:1] = summed[:, :W]
    out[1:2] = summed[:, W:]


def phase_tables():
    column = np.arange(NK)
    source, z, l = column // 8, column // 2 % 4, column % 2
    y, x, core = source // 8, source // 2 % 4, source % 2
    coordinates = (2 * z + y // 2, (y % 2) * 4 + x, 2 * core + l)
    tables = np.zeros((3, 2, FG, NK), np.float64)
    for axis, (size, where) in enumerate(zip((8, 8, 4), coordinates)):
        steps = np.arange(FG)[:, None] - (FG // size) * where[None, :]
        for cell in range(-size // 2, size // 2):
            angle = 2.0 * math.pi * ((cell * steps) % FG) / FG
            tables[axis, 0] += np.cos(angle) / size
            tables[axis, 1] += np.sin(angle) / size
    tables = np.concatenate([tables[:, 0], tables[:, 1]], -1)
    terms = []
    for _ in range(3):
        terms.append(tables.astype(jnp.bfloat16))
        tables = tables - terms[-1].astype(np.float64)
    return np.concatenate(terms, 1)


def call(kernel, shapes, specs, flops, vmem=16, **more):
    return pl.pallas_call(
        kernel,
        out_shape=shapes,
        in_specs=specs,
        cost_estimate=pl.CostEstimate(flops=flops, bytes_accessed=1 << 20, transcendentals=0),
        compiler_params=pltpu.CompilerParams(vmem_limit_bytes=vmem << 20),
        **more,
    )


def f32(*shape):
    return jax.ShapeDtypeStruct(shape, jnp.float32)


def spread(value):
    return lax.all_to_all(value, "z", 0, 0, tiled=True)


def shifted(values):
    arrived = [values[0]]
    for shift in (1, 2, 3):
        pairs = [(z, (z + shift) % 4) for z in range(4)]
        arrived.append(lax.ppermute(values[shift], "z", pairs))
    return arrived


def shards(
    coupling,
    gauge,
    kq_index,
    fine_coords,
    eig_right,
    eig_left,
    energy_k,
    energy_kq,
    occupied,
    frequency,
):
    along_z, along_y, along_x, core = (lax.axis_index(name) for name in KA)
    target = kq_index[lax.axis_index("pb") * 4 + along_z, 0]
    number = (((target >> 2) - (along_y * 4 + along_x)) & 7) + (
        (((target >> 5) - (along_y >> 1)) & 1) << 3
    )
    position = jnp.stack([along_z, along_y, along_x, core, target, number])
    planes = spread(jnp.broadcast_to(gauge[None], (4, 2, W, LANES)))
    products = call(right_kernel, f32(4, 2, 2, W, LANES), [VMEM, VMEM], 1 << 27)(coupling, gauge)
    products = spread(products)
    packs = call(pack_kernel, [f32(264, LANES)] * 4, [SMEM] + [VMEM] * 5, 1 << 20)(
        position, eig_left, eig_right, energy_k, energy_kq, occupied
    )
    branches = [functools.partial(translated, number=number) for number in range(16)]
    kept = lax.switch(number, branches, planes)
    swapped = lax.ppermute(kept, "core", [(0, 1), (1, 0)])
    pieces = call(left_kernel, f32(1024, LANES), [SMEM] + [VMEM] * 3, 1 << 27)(
        position, kept, swapped, products
    )
    columns = lax.all_to_all(pieces.reshape(32, 32, LANES), ("y", "x", "core"), 0, 0, tiled=True)
    packs = shifted(packs)
    coords = fine_coords.reshape(3, 4, 32, 2).transpose(0, 2, 1, 3).reshape(3, NK)
    high, low = call(
        phase_kernel,
        [jax.ShapeDtypeStruct((2 * NK, NK), jnp.bfloat16)] * 2,
        [VMEM, VMEM],
        1 << 28,
    )(coords, jnp.asarray(phase_tables()))
    fixed = pl.BlockSpec((2 * NK, NK), lambda i: (0, 0))
    fine = call(
        fourier_kernel,
        f32(32, 4, 8, LANES),
        [fixed, fixed, pl.BlockSpec((32, 16, LANES), lambda i: (0, i, 0))],
        1 << 28,
        grid=(2,),
        out_specs=pl.BlockSpec((32, 2, 8, LANES), lambda i: (0, i, 0, 0)),
    )(high, low, columns)
    blocks = lax.all_to_all(
        fine.reshape(32, 32, LANES), ("y", "x", "core"), 0, 0, tiled=True
    )
    terms = call(bloch_kernel, f32(16, 1, LANES), [SMEM, SMEM] + [VMEM] * 5, 1 << 27)(
        position, frequency, blocks.reshape(1024, LANES), *packs
    )
    terms = lax.all_to_all(terms, ("z", "pb"), 0, 0, tiled=True)
    return call(sum_kernel, f32(2, W), [VMEM], 1 << 12)(terms)


def solution(mesh):
    split = Mesh(mesh.devices.reshape(4, 4, 4, 2, mesh.shape["pb"]), (*KA, "pb"))
    return jax.shard_map(
        shards,
        mesh=split,
        in_specs=(
            P(KA, "pb", None, None, None),
            P(KA, None, None),
            P(None, KA),
            P(),
            P(KA, None, None),
            P(KA, "pb", None, None),
            P(KA, None),
            P(KA, "pb", None),
            P(KA, "pb", None),
            P("pb", None),
        ),
        out_specs=P(KA, None),
        check_vma=False,
    )
```

```python
import functools
import math

import jax
import jax.numpy as jnp
import numpy as np
from jax import lax
from jax.experimental import pallas as pl
from jax.experimental.pallas import tpu as pltpu
from jax.sharding import Mesh
from jax.sharding import PartitionSpec as P

FG = 32
W = 64
LANES = 128
NK = 256
BROADEN = 0.1
THERMAL = 0.05
KA = ("z", "y", "x", "core")
VMEM = pl.BlockSpec(memory_space=pltpu.VMEM)
SMEM = pl.BlockSpec(memory_space=pltpu.SMEM)


def halves(value):
    high = value.astype(jnp.bfloat16)
    low = (value - high.astype(jnp.float32)).astype(jnp.bfloat16)
    return high, low


def product(left, right, axes):
    left_high, left_low = left
    right_high, right_low = right
    return lax.dot_general(
        jnp.concatenate([left_high, left_high, left_low], axes[0]),
        jnp.concatenate([right_high, right_low, right_high], axes[1]),
        (((axes[0],), (axes[1],)), ((), ())),
        preferred_element_type=jnp.float32,
    )


def right_block(matrix):
    turned = signs(-1.0) * pltpu.roll(matrix, W, 1)
    high, low = halves(matrix)
    turned_high, turned_low = halves(turned)
    return jnp.concatenate([high, turned_high], 0), jnp.concatenate([low, turned_low], 0)


def signs(first):
    lane = lax.broadcasted_iota(jnp.int32, (1, LANES), 1)
    return jnp.where(lane < W, first, -first)


def apply_left(left, right_pair):
    both = product(halves(left), halves(right_pair), (0, 0))
    sign = signs(1.0)
    return [
        both[:W, at : at + LANES] + sign * pltpu.roll(both[W:, at : at + LANES], W, 1)
        for at in (0, LANES)
    ]


def translation(number):
    along_second, along_first = number % 8, number // 8
    pairs = []
    for y in range(4):
        for x in range(4):
            second = ((y % 2) * 4 + x + along_second) % 8
            first = (y // 2 + along_first) % 2
            pairs.append(((first * 2 + second // 4) * 4 + second % 4, y * 4 + x))
    return pairs


def translated(value, number):
    pairs = translation(number)
    if all(source == target for source, target in pairs):
        return value
    return lax.ppermute(value, ("y", "x"), pairs)


def prepare_kernel(
    coupling, gauge, coords, tables, eig_left, eig_right, energy_k, energy_kq, occupied, *outs
):
    right_part(coupling, gauge, outs[0])
    pack_part(eig_left, eig_right, energy_k, energy_kq, occupied, outs[3:])
    phase_part(coords, tables, outs[1], outs[2])


def right_part(coupling, gauge, out):
    for k in range(2):
        rows = coupling[k].reshape(-1, LANES)
        result = product(halves(rows), right_block(gauge[k]), (1, 0)).reshape(4, 2, W, LANES)
        for q in range(4):
            out[q, k] = result[q]


def pack_part(eig_left, eig_right, energy_k, energy_kq, occupied, outs):
    for shift, out in enumerate(outs):
        q = (lax.axis_index("z") + shift) & 3
        for f in range(2):
            out[f * W : f * W + W] = eig_left[f, q]
            out[LANES + f * W : LANES + f * W + W] = eig_right[f]
            filled = occupied[f, pl.ds(q, 1), :].astype(jnp.float32)
            row = 2 * LANES + f
            out[row : row + 1] = jnp.concatenate([energy_k[f : f + 1], energy_k[f : f + 1]], -1)
            out[row + 2 : row + 3] = jnp.concatenate([energy_kq[f, pl.ds(q, 1), :], filled], -1)
        out[2 * LANES + 4 :] = jnp.zeros((4, LANES), jnp.float32)


def left_kernel(target, kept, swapped, products, out):
    along_z, along_y, core = (lax.axis_index(name) for name in ("z", "y", "core"))
    target = target[0]
    first = (target >> 5) - 2 * along_z - (along_y >> 1)
    carry = ((along_y >> 1) + (first & 7)) >> 1
    wanniers = []
    for l in range(2):
        third = (target + l) & 3
        mine = (third >> 1) == core
        for z in range(4):
            plane = (z + carry - along_z + 4) & 3
            gauge = jnp.where(mine, kept[plane, third & 1], swapped[plane, third & 1])
            pair = jnp.concatenate([products[z, l, 0], products[z, l, 1]], -1)
            wanniers.append((l, z, apply_left(gauge, pair)))
    for l, z, both in wanniers:
        for b, wannier in enumerate(both):
            for part in range(2):
                start = (part * 2 + b) * 8 + z * 2 + l
                out[pl.ds(start, 32, stride=32), :] = wannier[part * 32 : part * 32 + 32]


def phase_part(coords, tables, high, low):
    source = lax.broadcasted_iota(jnp.int32, (NK, NK), 0)
    row = lax.broadcasted_iota(jnp.int32, (NK, NK), 1)
    wanted = (((row >> 1) & 3) << 6) + ((row >> 3) << 1) + (row & 1)
    turn = (source == wanted).astype(jnp.float32).astype(jnp.bfloat16)
    points = coords[...].astype(jnp.float32).astype(jnp.bfloat16)
    coords = jnp.dot(points, turn, preferred_element_type=jnp.float32)
    real, imag = None, None
    divisions = lax.broadcasted_iota(jnp.int32, (FG, NK), 0).astype(jnp.float32)
    for axis in range(3):
        onehot = (divisions == coords[axis : axis + 1, :]).astype(jnp.float32)
        onehot = onehot.astype(jnp.bfloat16)
        factor = lax.dot_general(
            jnp.concatenate([onehot] * 3, 0),
            tables[axis],
            (((0,), (0,)), ((), ())),
            preferred_element_type=jnp.float32,
        )
        factor = factor[:, :NK], factor[:, NK:]
        if real is None:
            real, imag = factor
        else:
            real, imag = (
                real * factor[0] - imag * factor[1],
                real * factor[1] + imag * factor[0],
            )
    for row, part in enumerate((real, imag)):
        part_high, part_low = halves(part)
        high[row * NK : row * NK + NK] = part_high
        low[row * NK : row * NK + NK] = part_low


def fourier_kernel(high, low, columns, out):
    parts = [columns[:, at : at + 8, :].reshape(NK, LANES) for at in (0, 8)]
    result = product((high[...], low[...]), halves(jnp.concatenate(parts, -1)), (1, 0))
    sign = signs(-1.0)
    for c in range(2):
        at = c * LANES
        rolled = pltpu.roll(result[NK:, at : at + LANES], W, 1)
        value = result[:NK, at : at + LANES] + sign * rolled
        out[:, c] = value.reshape(32, 8, LANES)


def bloch_kernel(frequency, arrived, *packs_and_out):
    packs, out = packs_and_out[:4], packs_and_out[4]
    lane = lax.broadcasted_iota(jnp.int32, (1, LANES), 1)
    first = lane < W
    phonons = [
        jnp.full((1, LANES), frequency[lax.axis_index("z"), b], jnp.float32) for b in range(2)
    ]
    boses = [1.0 / (jnp.exp(phonon / THERMAL) - 1.0) for phonon in phonons]
    scales = [1.0 / (2.0 * phonon) for phonon in phonons]
    pairs = []
    for shift, pack in enumerate(packs):
        plane = (lax.axis_index("z") - shift + 4) & 3
        for f in range(2):
            rows = [
                arrived[pl.ds((part * 2 + b) * 8 + plane * 2 + f, 32, stride=32), :]
                for b in range(2)
                for part in range(2)
            ]
            eig_right = pack[LANES + f * W : LANES + f * W + W]
            half = product(halves(jnp.concatenate(rows, 0)), right_block(eig_right), (1, 0))
            pairs.append(jnp.concatenate([half[:W], half[W:]], -1))
    squares = []
    for shift, pack in enumerate(packs):
        for f in range(2):
            blochs = apply_left(pack[f * W : f * W + W], pairs[shift * 2 + f])
            squares.append([bloch * bloch for bloch in blochs])
    for shift, pack in enumerate(packs):
        tail = pack[2 * LANES :]
        energies = jnp.where(first, tail[0:1], tail[1:2])
        states = tail.T
        energy_left = jnp.where(first, states[:W, 2:3], states[:W, 3:4])
        filled = jnp.where(first, states[W:, 2:3], states[W:, 3:4])
        gap = energies - energy_left
        total = jnp.zeros((W, LANES), jnp.float32)
        for b, (phonon, bose) in enumerate(zip(phonons, boses)):
            up = gap + phonon
            down = gap - phonon
            up_square = up * up + BROADEN * BROADEN
            down_square = down * down + BROADEN * BROADEN
            terms = (bose + filled) * up * down_square + (bose + 1.0 - filled) * down * up_square
            one, two = squares[shift * 2][b], squares[shift * 2 + 1][b]
            strength = jnp.where(first, one, two) + pltpu.roll(jnp.where(first, two, one), W, 1)
            total = total + strength * scales[b] * terms / (up_square * down_square)
        summed = jnp.sum(total, axis=0, keepdims=True) * (1.0 / 1024.0)
        plane = (lax.axis_index("z") - shift + 4) & 3
        for group in range(4):
            out[plane * 4 + group] = summed


def sum_kernel(terms, out):
    summed = jnp.sum(terms[...], axis=0)
    out[0:1] = summed[:, :W]
    out[1:2] = summed[:, W:]


def phase_tables():
    column = np.arange(NK)
    source, z, l = column // 8, column // 2 % 4, column % 2
    y, x, core = source // 8, source // 2 % 4, source % 2
    coordinates = (2 * z + y // 2, (y % 2) * 4 + x, 2 * core + l)
    tables = np.zeros((3, 2, FG, NK), np.float64)
    for axis, (size, where) in enumerate(zip((8, 8, 4), coordinates)):
        steps = np.arange(FG)[:, None] - (FG // size) * where[None, :]
        for cell in range(-size // 2, size // 2):
            angle = 2.0 * math.pi * ((cell * steps) % FG) / FG
            tables[axis, 0] += np.cos(angle) / size
            tables[axis, 1] += np.sin(angle) / size
    tables = np.concatenate([tables[:, 0], tables[:, 1]], -1)
    terms = []
    for _ in range(3):
        terms.append(tables.astype(jnp.bfloat16))
        tables = tables - terms[-1].astype(np.float64)
    return np.concatenate(terms, 1)


def call(kernel, shapes, specs, flops, vmem=16, **more):
    return pl.pallas_call(
        kernel,
        out_shape=shapes,
        in_specs=specs,
        cost_estimate=pl.CostEstimate(flops=flops, bytes_accessed=1 << 20, transcendentals=0),
        compiler_params=pltpu.CompilerParams(vmem_limit_bytes=vmem << 20),
        **more,
    )


def f32(*shape):
    return jax.ShapeDtypeStruct(shape, jnp.float32)


def spread(value):
    return lax.all_to_all(value, "z", 0, 0, tiled=True)


def shifted(values):
    arrived = [values[0]]
    for shift in (1, 2, 3):
        pairs = [(z, (z + shift) % 4) for z in range(4)]
        arrived.append(lax.ppermute(values[shift], "z", pairs))
    return arrived


def shards(
    coupling,
    gauge,
    kq_index,
    fine_coords,
    eig_right,
    eig_left,
    energy_k,
    energy_kq,
    occupied,
    frequency,
):
    along_z, along_y, along_x, _ = (lax.axis_index(name) for name in KA)
    target = kq_index[lax.axis_index("pb") * 4 + along_z, 0]
    number = (((target >> 2) - (along_y * 4 + along_x)) & 7) + (
        (((target >> 5) - (along_y >> 1)) & 1) << 3
    )
    planes = [gauge]
    for ahead in (1, 2, 15):
        ring = [place % 4 * 4 + place // 4 for place in range(16)]
        pairs = [(ring[(place + ahead) % 16], ring[place]) for place in range(16)]
        planes.append(lax.ppermute(gauge, ("z", "pb"), pairs))
    planes = jnp.stack(planes)
    products, high, low, *packs = call(
        prepare_kernel,
        [f32(4, 2, 2, W, LANES)]
        + [jax.ShapeDtypeStruct((2 * NK, NK), jnp.bfloat16)] * 2
        + [f32(264, LANES)] * 4,
        [VMEM] * 9,
        1 << 27,
    )(
        *(
            pltpu.with_memory_space_constraint(value, pltpu.HBM)
            for value in (
                coupling,
                gauge,
                fine_coords,
                jnp.asarray(phase_tables()),
                eig_left,
                eig_right,
                energy_k,
                energy_kq,
                occupied,
            )
        )
    )
    products = spread(products)
    branches = [functools.partial(translated, number=number) for number in range(16)]
    kept = lax.switch(number, branches, planes)
    swapped = lax.ppermute(kept, "core", [(0, 1), (1, 0)])
    pieces = call(left_kernel, f32(1024, LANES), [SMEM] + [VMEM] * 3, 1 << 27)(
        target.reshape(1), kept, swapped, products
    )
    columns = lax.all_to_all(pieces.reshape(32, 32, LANES), ("y", "x", "core"), 0, 0, tiled=True)
    packs = shifted(packs)
    fixed = pl.BlockSpec((2 * NK, NK), lambda i: (0, 0))
    fine = call(
        fourier_kernel,
        f32(32, 4, 8, LANES),
        [fixed, fixed, pl.BlockSpec((32, 16, LANES), lambda i: (0, i, 0))],
        1 << 28,
        grid=(2,),
        out_specs=pl.BlockSpec((32, 2, 8, LANES), lambda i: (0, i, 0, 0)),
    )(high, low, columns)
    blocks = lax.all_to_all(
        fine.reshape(32, 32, LANES), ("y", "x", "core"), 0, 0, tiled=True
    )
    terms = call(bloch_kernel, f32(16, 1, LANES), [SMEM] + [VMEM] * 5, 1 << 27)(
        frequency, blocks.reshape(1024, LANES), *packs
    )
    terms = lax.all_to_all(terms, ("z", "pb"), 0, 0, tiled=True)
    return call(sum_kernel, f32(2, W), [VMEM], 1 << 12)(terms)


def solution(mesh):
    split = Mesh(mesh.devices.reshape(4, 4, 4, 2, mesh.shape["pb"]), (*KA, "pb"))
    return jax.shard_map(
        shards,
        mesh=split,
        in_specs=(
            P(KA, "pb", None, None, None),
            P(KA, None, None),
            P(None, KA),
            P(),
            P(KA, None, None),
            P(KA, "pb", None, None),
            P(KA, None),
            P(KA, "pb", None),
            P(KA, "pb", None),
            P("pb", None),
        ),
        out_specs=P(KA, None),
        check_vma=False,
    )
```

```python
import functools
import math

import jax
import jax.numpy as jnp
import numpy as np
from jax import lax
from jax.experimental import pallas as pl
from jax.experimental.pallas import tpu as pltpu
from jax.sharding import Mesh
from jax.sharding import PartitionSpec as P

FG = 32
W = 64
LANES = 128
NK = 256
BROADEN = 0.1
THERMAL = 0.05
KA = ("z", "y", "x", "core")
VMEM = pl.BlockSpec(memory_space=pltpu.VMEM)
SMEM = pl.BlockSpec(memory_space=pltpu.SMEM)


def halves(value):
    high = value.astype(jnp.bfloat16)
    low = (value - high.astype(jnp.float32)).astype(jnp.bfloat16)
    return high, low


def product(left, right, axes):
    left_high, left_low = left
    right_high, right_low = right
    return lax.dot_general(
        jnp.concatenate([left_high, left_high, left_low], axes[0]),
        jnp.concatenate([right_high, right_low, right_high], axes[1]),
        (((axes[0],), (axes[1],)), ((), ())),
        preferred_element_type=jnp.float32,
    )


def right_block(matrix):
    turned = signs(-1.0) * pltpu.roll(matrix, W, 1)
    high, low = halves(matrix)
    turned_high, turned_low = halves(turned)
    return jnp.concatenate([high, turned_high], 0), jnp.concatenate([low, turned_low], 0)


def signs(first):
    lane = lax.broadcasted_iota(jnp.int32, (1, LANES), 1)
    return jnp.where(lane < W, first, -first)


def apply_left(left, right):
    both = product(halves(left), halves(right), (0, 0))
    sign = signs(1.0)
    return [
        both[:W, at : at + LANES] + sign * pltpu.roll(both[W:, at : at + LANES], W, 1)
        for at in range(0, right.shape[1], LANES)
    ]


def translation(number):
    along_second, along_first = number % 8, number // 8
    pairs = []
    for y in range(4):
        for x in range(4):
            second = ((y % 2) * 4 + x + along_second) % 8
            first = (y // 2 + along_first) % 2
            pairs.append(((first * 2 + second // 4) * 4 + second % 4, y * 4 + x))
    return pairs


def translated(value, number):
    pairs = translation(number)
    if all(source == target for source, target in pairs):
        return value
    return lax.ppermute(value, ("y", "x"), pairs)


def right_kernel(coupling, gauge, out):
    for k in range(2):
        block = right_block(gauge[k])
        rows = coupling[k].reshape(-1, LANES)
        result = product(halves(rows), block, (1, 0)).reshape(8, W, LANES)
        for column in range(8):
            out[column, k] = result[column]


def pack_kernel(position, eig_left, eig_right, energy_k, energy_kq, occupied, *outs):
    for shift, out in enumerate(outs):
        q = (position[0] + shift) & 3
        for f in range(2):
            out[f * W : f * W + W] = eig_left[f, q]
            out[LANES + f * W : LANES + f * W + W] = eig_right[f]
            filled = occupied[f, pl.ds(q, 1), :].astype(jnp.float32)
            row = 2 * LANES + f
            out[row : row + 1] = jnp.concatenate([energy_k[f : f + 1], energy_k[f : f + 1]], -1)
            out[row + 2 : row + 3] = jnp.concatenate([energy_kq[f, pl.ds(q, 1), :], filled], -1)
        out[2 * LANES + 4 :] = jnp.zeros((4, LANES), jnp.float32)


def left_kernel(position, kept, swapped, products, out):
    core, target = position[3], position[4]
    first = (target >> 5) - 2 * position[0] - (position[1] >> 1)
    carry = ((position[1] >> 1) + (first & 7)) >> 1
    wanniers = []
    for place in range(4):
        third = (target - 2 * core + place) & 3
        mine = (third >> 1) == core
        for z in range(4):
            plane = (z + carry) & 3
            gauge = jnp.where(mine, kept[plane, third & 1], swapped[plane, third & 1])
            wannier = apply_left(gauge, products[z * 2 + place // 2, place % 2])[0]
            wanniers.append((z * 4 + place, wannier))
    for start, wannier in wanniers:
        for part in range(4):
            rows = wannier[part * 16 : part * 16 + 16]
            out[pl.ds(part * 16 + start, 16, stride=64), :] = rows


def phase_kernel(coords, tables, high, low):
    real, imag = None, None
    divisions = lax.broadcasted_iota(jnp.int32, (FG, NK), 0)
    for axis in range(3):
        onehot = (divisions == coords[axis : axis + 1, :]).astype(jnp.float32)
        onehot = onehot.astype(jnp.bfloat16)
        factor = lax.dot_general(
            jnp.concatenate([onehot] * 3, 0),
            tables[axis],
            (((0,), (0,)), ((), ())),
            preferred_element_type=jnp.float32,
        )
        factor = factor[:, :NK], factor[:, NK:]
        if real is None:
            real, imag = factor
        else:
            real, imag = (
                real * factor[0] - imag * factor[1],
                real * factor[1] + imag * factor[0],
            )
    for row, part in enumerate((real, imag)):
        part_high, part_low = halves(part)
        high[row * NK : row * NK + NK] = part_high
        low[row * NK : row * NK + NK] = part_low


def fourier_kernel(high, low, columns, out):
    parts = [columns[:, at : at + 16, :].reshape(NK, LANES) for at in (0, 16)]
    result = product((high[...], low[...]), halves(jnp.concatenate(parts, -1)), (1, 0))
    sign = signs(-1.0)
    for c in range(2):
        at = c * LANES
        rolled = pltpu.roll(result[NK:, at : at + LANES], W, 1)
        value = result[:NK, at : at + LANES] + sign * rolled
        out[:, c] = value.reshape(32, 8, LANES)


def bloch_kernel(position, frequency, arrived, *packs_and_out):
    packs, out = packs_and_out[:4], packs_and_out[4]
    lane = lax.broadcasted_iota(jnp.int32, (1, LANES), 1)
    first = lane < W
    phonons = [
        jnp.full((1, LANES), frequency[position[0], b], jnp.float32) for b in range(2)
    ]
    boses = [1.0 / (jnp.exp(phonon / THERMAL) - 1.0) for phonon in phonons]
    scales = [1.0 / (2.0 * phonon) for phonon in phonons]
    pairs = []
    for shift, pack in enumerate(packs):
        plane = (position[0] - shift + 4) & 3
        for f in range(2):
            rows = [
                arrived[pl.ds(b * 32 + part * 8 + plane * 2 + f, 16, stride=64), :]
                for b in range(2)
                for part in range(4)
            ]
            eig_right = pack[LANES + f * W : LANES + f * W + W]
            half = product(halves(jnp.concatenate(rows, 0)), right_block(eig_right), (1, 0))
            pairs.append(jnp.concatenate([half[:W], half[W:]], -1))
    squares = []
    for shift, pack in enumerate(packs):
        for f in range(2):
            blochs = apply_left(pack[f * W : f * W + W], pairs[shift * 2 + f])
            squares.append([bloch * bloch for bloch in blochs])
    for shift, pack in enumerate(packs):
        tail = pack[2 * LANES :]
        energies = jnp.where(first, tail[0:1], tail[1:2])
        states = tail.T
        energy_left = jnp.where(first, states[:W, 2:3], states[:W, 3:4])
        filled = jnp.where(first, states[W:, 2:3], states[W:, 3:4])
        gap = energies - energy_left
        total = jnp.zeros((W, LANES), jnp.float32)
        for b, (phonon, bose) in enumerate(zip(phonons, boses)):
            up = gap + phonon
            down = gap - phonon
            up_square = up * up + BROADEN * BROADEN
            down_square = down * down + BROADEN * BROADEN
            terms = (bose + filled) * up * down_square + (bose + 1.0 - filled) * down * up_square
            one, two = squares[shift * 2][b], squares[shift * 2 + 1][b]
            strength = jnp.where(first, one, two) + pltpu.roll(jnp.where(first, two, one), W, 1)
            total = total + strength * scales[b] * terms / (up_square * down_square)
        summed = jnp.sum(total, axis=0, keepdims=True) * (1.0 / 1024.0)
        plane = (position[0] - shift + 4) & 3
        for group in range(4):
            out[plane * 4 + group] = summed


def sum_kernel(terms, out):
    summed = jnp.sum(terms[...], axis=0)
    out[0:1] = summed[:, :W]
    out[1:2] = summed[:, W:]


def phase_tables():
    column = np.arange(NK)
    source, z, place = column // 16, column // 4 % 4, column % 4
    y, x = source // 4, source % 4
    coordinates = (2 * z + y // 2, (y % 2) * 4 + x, place)
    tables = np.zeros((3, 2, FG, NK), np.float64)
    for axis, (size, where) in enumerate(zip((8, 8, 4), coordinates)):
        steps = np.arange(FG)[:, None] - (FG // size) * where[None, :]
        for cell in range(-size // 2, size // 2):
            angle = 2.0 * math.pi * ((cell * steps) % FG) / FG
            tables[axis, 0] += np.cos(angle) / size
            tables[axis, 1] += np.sin(angle) / size
    tables = np.concatenate([tables[:, 0], tables[:, 1]], -1)
    terms = []
    for _ in range(3):
        terms.append(tables.astype(jnp.bfloat16))
        tables = tables - terms[-1].astype(np.float64)
    return np.concatenate(terms, 1)


def call(kernel, shapes, specs, flops, vmem=16, **more):
    return pl.pallas_call(
        kernel,
        out_shape=shapes,
        in_specs=specs,
        cost_estimate=pl.CostEstimate(flops=flops, bytes_accessed=1 << 20, transcendentals=0),
        compiler_params=pltpu.CompilerParams(vmem_limit_bytes=vmem << 20),
        **more,
    )


def f32(*shape):
    return jax.ShapeDtypeStruct(shape, jnp.float32)


def spread(value, axes):
    return lax.all_to_all(value, axes, 0, 0, tiled=True)


def shifted(values):
    arrived = [values[0]]
    for shift in (1, 2, 3):
        pairs = [(z, (z + shift) % 4) for z in range(4)]
        arrived.append(lax.ppermute(values[shift], "z", pairs))
    return arrived


def shards(
    coupling,
    gauge,
    kq_index,
    fine_coords,
    eig_right,
    eig_left,
    energy_k,
    energy_kq,
    occupied,
    frequency,
):
    along_z, along_y, along_x, core = (lax.axis_index(name) for name in KA)
    target = kq_index[lax.axis_index("pb") * 4 + along_z, 0]
    number = (((target >> 2) - (along_y * 4 + along_x)) & 7) + (
        (((target >> 5) - (along_y >> 1)) & 1) << 3
    )
    position = jnp.stack([along_z, along_y, along_x, core, target, number])
    planes = spread(jnp.broadcast_to(gauge[None], (4, 2, W, LANES)), "z")
    products = call(right_kernel, f32(8, 2, W, LANES), [VMEM, VMEM], 1 << 27)(
        coupling, gauge
    )
    products = spread(products, ("z", "core"))
    packs = call(pack_kernel, [f32(264, LANES)] * 4, [SMEM] + [VMEM] * 5, 1 << 20)(
        position, eig_left, eig_right, energy_k, energy_kq, occupied
    )
    branches = [functools.partial(translated, number=number) for number in range(16)]
    kept = lax.switch(number, branches, planes)
    swapped = lax.ppermute(kept, "core", [(0, 1), (1, 0)])
    pieces = call(left_kernel, f32(1024, LANES), [SMEM] + [VMEM] * 3, 1 << 27)(
        position, kept, swapped, products
    )
    columns = lax.all_to_all(
        pieces.reshape(16, 64, LANES), ("y", "x"), 0, 0, tiled=True
    )
    packs = shifted(packs)
    coords = fine_coords.reshape(3, 4, 32, 2).transpose(0, 2, 1, 3).reshape(3, NK)
    high, low = call(
        phase_kernel,
        [jax.ShapeDtypeStruct((2 * NK, NK), jnp.bfloat16)] * 2,
        [VMEM, VMEM],
        1 << 28,
    )(coords, jnp.asarray(phase_tables()))
    fixed = pl.BlockSpec((2 * NK, NK), lambda i: (0, 0))
    fine = call(
        fourier_kernel,
        f32(32, 4, 8, LANES),
        [fixed, fixed, pl.BlockSpec((16, 32, LANES), lambda i: (0, i, 0))],
        1 << 28,
        grid=(2,),
        out_specs=pl.BlockSpec((32, 2, 8, LANES), lambda i: (0, i, 0, 0)),
    )(high, low, columns)
    blocks = lax.all_to_all(
        fine.reshape(32, 32, LANES), ("y", "x", "core"), 0, 0, tiled=True
    )
    terms = call(bloch_kernel, f32(16, 1, LANES), [SMEM, SMEM] + [VMEM] * 5, 1 << 27)(
        position, frequency, blocks.reshape(1024, LANES), *packs
    )
    terms = lax.all_to_all(terms, ("z", "pb"), 0, 0, tiled=True)
    return call(sum_kernel, f32(2, W), [VMEM], 1 << 12)(terms)


def solution(mesh):
    split = Mesh(mesh.devices.reshape(4, 4, 4, 2, mesh.shape["pb"]), (*KA, "pb"))
    return jax.shard_map(
        shards,
        mesh=split,
        in_specs=(
            P(KA, "pb", None, None, None),
            P(KA, None, None),
            P(None, KA),
            P(),
            P(KA, None, None),
            P(KA, "pb", None, None),
            P(KA, None),
            P(KA, "pb", None),
            P(KA, "pb", None),
            P("pb", None),
        ),
        out_specs=P(KA, None),
        check_vma=False,
    )
```

```python
import functools
import math

import jax
import jax.numpy as jnp
import numpy as np
from jax import lax
from jax.experimental import pallas as pl
from jax.experimental.pallas import tpu as pltpu
from jax.sharding import Mesh
from jax.sharding import PartitionSpec as P

FG = 32
W = 64
LANES = 128
NK = 256
BROADEN = 0.1
THERMAL = 0.05
KA = ("z", "y", "x", "core")
VMEM = pl.BlockSpec(memory_space=pltpu.VMEM)
SMEM = pl.BlockSpec(memory_space=pltpu.SMEM)


def halves(value):
    high = value.astype(jnp.bfloat16)
    low = (value - high.astype(jnp.float32)).astype(jnp.bfloat16)
    return high, low


def product(left, right, axes):
    left_high, left_low = left
    right_high, right_low = right
    return lax.dot_general(
        jnp.concatenate([left_high, left_high, left_low], axes[0]),
        jnp.concatenate([right_high, right_low, right_high], axes[1]),
        (((axes[0],), (axes[1],)), ((), ())),
        preferred_element_type=jnp.float32,
    )


def right_block(matrix):
    turned = signs(-1.0) * pltpu.roll(matrix, W, 1)
    high, low = halves(matrix)
    turned_high, turned_low = halves(turned)
    return jnp.concatenate([high, turned_high], 0), jnp.concatenate([low, turned_low], 0)


def signs(first):
    lane = lax.broadcasted_iota(jnp.int32, (1, LANES), 1)
    return jnp.where(lane < W, first, -first)


def apply_left(left, right_pair):
    both = product(halves(left), halves(right_pair), (0, 0))
    sign = signs(1.0)
    return [
        both[:W, at : at + LANES] + sign * pltpu.roll(both[W:, at : at + LANES], W, 1)
        for at in (0, LANES)
    ]


def translation(number):
    along_second, along_first = number % 8, number // 8
    pairs = []
    for y in range(4):
        for x in range(4):
            second = ((y % 2) * 4 + x + along_second) % 8
            first = (y // 2 + along_first) % 2
            pairs.append(((first * 2 + second // 4) * 4 + second % 4, y * 4 + x))
    return pairs


def translated(value, number):
    pairs = translation(number)
    if all(source == target for source, target in pairs):
        return value
    return lax.ppermute(value, ("y", "x"), pairs)


def right_kernel(coupling, gauge, kq, out, number, target):
    along_z, along_y, along_x, pb = (lax.axis_index(name) for name in ("z", "y", "x", "pb"))
    point = kq[0, pb * 4 + along_z]
    target[0] = point
    number[0] = (((point >> 2) - (along_y * 4 + along_x)) & 7) + (
        (((point >> 5) - (along_y >> 1)) & 1) << 3
    )
    for k in range(2):
        rows = coupling[k].reshape(-1, LANES)
        result = product(halves(rows), right_block(gauge[k]), (1, 0)).reshape(4, 2, W, LANES)
        for q in range(4):
            out[q, k] = result[q]


def owners_kernel(
    coords, tables, eig_left, eig_right, energy_k, energy_kq, occupied, high, low, *outs
):
    pack_part(eig_left, eig_right, energy_k, energy_kq, occupied, outs)
    phase_part(coords, tables, high, low)


def pack_part(eig_left, eig_right, energy_k, energy_kq, occupied, outs):
    for shift, out in enumerate(outs):
        q = (lax.axis_index("z") + shift) & 3
        for f in range(2):
            out[f * W : f * W + W] = eig_left[f, q]
            out[LANES + f * W : LANES + f * W + W] = eig_right[f]
            filled = occupied[f, pl.ds(q, 1), :].astype(jnp.float32)
            row = 2 * LANES + f
            out[row : row + 1] = jnp.concatenate([energy_k[f : f + 1], energy_k[f : f + 1]], -1)
            out[row + 2 : row + 3] = jnp.concatenate([energy_kq[f, pl.ds(q, 1), :], filled], -1)
        out[2 * LANES + 4 :] = jnp.zeros((4, LANES), jnp.float32)


def left_kernel(target, kept, swapped, products, out):
    along_z, along_y, core = (lax.axis_index(name) for name in ("z", "y", "core"))
    target = target[0]
    first = (target >> 5) - 2 * along_z - (along_y >> 1)
    carry = ((along_y >> 1) + (first & 7)) >> 1
    wanniers = []
    for l in range(2):
        third = (target + l) & 3
        mine = (third >> 1) == core
        for z in range(4):
            plane = (z + carry - along_z + 4) & 3
            gauge = jnp.where(mine, kept[plane, third & 1], swapped[plane, third & 1])
            pair = jnp.concatenate([products[z, l, 0], products[z, l, 1]], -1)
            wanniers.append((l, z, apply_left(gauge, pair)))
    for l, z, both in wanniers:
        for b, wannier in enumerate(both):
            for part in range(2):
                start = (part * 2 + b) * 8 + z * 2 + l
                out[pl.ds(start, 32, stride=32), :] = wannier[part * 32 : part * 32 + 32]


def phase_part(coords, tables, high, low):
    source = lax.broadcasted_iota(jnp.int32, (NK, NK), 0)
    row = lax.broadcasted_iota(jnp.int32, (NK, NK), 1)
    wanted = (((row >> 1) & 3) << 6) + ((row >> 3) << 1) + (row & 1)
    turn = (source == wanted).astype(jnp.float32).astype(jnp.bfloat16)
    points = coords[...].astype(jnp.float32).astype(jnp.bfloat16)
    coords = jnp.dot(points, turn, preferred_element_type=jnp.float32)
    real, imag = None, None
    divisions = lax.broadcasted_iota(jnp.int32, (FG, NK), 0).astype(jnp.float32)
    for axis in range(3):
        onehot = (divisions == coords[axis : axis + 1, :]).astype(jnp.float32)
        onehot = onehot.astype(jnp.bfloat16)
        factor = lax.dot_general(
            jnp.concatenate([onehot] * 3, 0),
            tables[axis],
            (((0,), (0,)), ((), ())),
            preferred_element_type=jnp.float32,
        )
        factor = factor[:, :NK], factor[:, NK:]
        if real is None:
            real, imag = factor
        else:
            real, imag = (
                real * factor[0] - imag * factor[1],
                real * factor[1] + imag * factor[0],
            )
    for row, part in enumerate((real, imag)):
        part_high, part_low = halves(part)
        high[row * NK : row * NK + NK] = part_high
        low[row * NK : row * NK + NK] = part_low


def fourier_kernel(high, low, columns, out):
    parts = [columns[:, at : at + 8, :].reshape(NK, LANES) for at in (0, 8)]
    result = product((high[...], low[...]), halves(jnp.concatenate(parts, -1)), (1, 0))
    sign = signs(-1.0)
    for c in range(2):
        at = c * LANES
        rolled = pltpu.roll(result[NK:, at : at + LANES], W, 1)
        value = result[:NK, at : at + LANES] + sign * rolled
        out[:, c] = value.reshape(32, 8, LANES)


def bloch_kernel(frequency, arrived, *packs_and_out):
    packs, out = packs_and_out[:4], packs_and_out[4]
    lane = lax.broadcasted_iota(jnp.int32, (1, LANES), 1)
    first = lane < W
    phonons = [
        jnp.full((1, LANES), frequency[lax.axis_index("z"), b], jnp.float32) for b in range(2)
    ]
    boses = [1.0 / (jnp.exp(phonon / THERMAL) - 1.0) for phonon in phonons]
    scales = [1.0 / (2.0 * phonon) for phonon in phonons]
    pairs = []
    for shift, pack in enumerate(packs):
        plane = (lax.axis_index("z") - shift + 4) & 3
        for f in range(2):
            rows = [
                arrived[pl.ds((part * 2 + b) * 8 + plane * 2 + f, 32, stride=32), :]
                for b in range(2)
                for part in range(2)
            ]
            eig_right = pack[LANES + f * W : LANES + f * W + W]
            half = product(halves(jnp.concatenate(rows, 0)), right_block(eig_right), (1, 0))
            pairs.append(jnp.concatenate([half[:W], half[W:]], -1))
    squares = []
    for shift, pack in enumerate(packs):
        for f in range(2):
            blochs = apply_left(pack[f * W : f * W + W], pairs[shift * 2 + f])
            squares.append([bloch * bloch for bloch in blochs])
    for shift, pack in enumerate(packs):
        tail = pack[2 * LANES :]
        energies = jnp.where(first, tail[0:1], tail[1:2])
        states = tail.T
        energy_left = jnp.where(first, states[:W, 2:3], states[:W, 3:4])
        filled = jnp.where(first, states[W:, 2:3], states[W:, 3:4])
        gap = energies - energy_left
        total = jnp.zeros((W, LANES), jnp.float32)
        for b, (phonon, bose) in enumerate(zip(phonons, boses)):
            up = gap + phonon
            down = gap - phonon
            up_square = up * up + BROADEN * BROADEN
            down_square = down * down + BROADEN * BROADEN
            terms = (bose + filled) * up * down_square + (bose + 1.0 - filled) * down * up_square
            one, two = squares[shift * 2][b], squares[shift * 2 + 1][b]
            strength = jnp.where(first, one, two) + pltpu.roll(jnp.where(first, two, one), W, 1)
            total = total + strength * scales[b] * terms / (up_square * down_square)
        summed = jnp.sum(total, axis=0, keepdims=True) * (1.0 / 1024.0)
        plane = (lax.axis_index("z") - shift + 4) & 3
        for group in range(4):
            out[plane * 4 + group] = summed


def sum_kernel(terms, out):
    summed = jnp.sum(terms[...], axis=0)
    out[0:1] = summed[:, :W]
    out[1:2] = summed[:, W:]


def phase_tables():
    column = np.arange(NK)
    source, z, l = column // 8, column // 2 % 4, column % 2
    y, x, core = source // 8, source // 2 % 4, source % 2
    coordinates = (2 * z + y // 2, (y % 2) * 4 + x, 2 * core + l)
    tables = np.zeros((3, 2, FG, NK), np.float64)
    for axis, (size, where) in enumerate(zip((8, 8, 4), coordinates)):
        steps = np.arange(FG)[:, None] - (FG // size) * where[None, :]
        for cell in range(-size // 2, size // 2):
            angle = 2.0 * math.pi * ((cell * steps) % FG) / FG
            tables[axis, 0] += np.cos(angle) / size
            tables[axis, 1] += np.sin(angle) / size
    tables = np.concatenate([tables[:, 0], tables[:, 1]], -1)
    terms = []
    for _ in range(3):
        terms.append(tables.astype(jnp.bfloat16))
        tables = tables - terms[-1].astype(np.float64)
    return np.concatenate(terms, 1)


def call(kernel, shapes, specs, flops, vmem=16, **more):
    return pl.pallas_call(
        kernel,
        out_shape=shapes,
        in_specs=specs,
        cost_estimate=pl.CostEstimate(flops=flops, bytes_accessed=1 << 20, transcendentals=0),
        compiler_params=pltpu.CompilerParams(vmem_limit_bytes=vmem << 20),
        **more,
    )


def f32(*shape):
    return jax.ShapeDtypeStruct(shape, jnp.float32)


def spread(value):
    return lax.all_to_all(value, "z", 0, 0, tiled=True)


def in_hbm(value):
    return pltpu.with_memory_space_constraint(value, pltpu.HBM)


def shifted(values):
    arrived = [values[0]]
    for shift in (1, 2, 3):
        pairs = [(z, (z + shift) % 4) for z in range(4)]
        arrived.append(lax.ppermute(values[shift], "z", pairs))
    return arrived


def shards(
    coupling,
    gauge,
    kq_index,
    fine_coords,
    eig_right,
    eig_left,
    energy_k,
    energy_kq,
    occupied,
    frequency,
):
    along_z, along_y, along_x, core = (lax.axis_index(name) for name in KA)
    planes = [gauge]
    for ahead in (1, 2, 15):
        ring = [place % 4 * 4 + place // 4 for place in range(16)]
        pairs = [(ring[(place + ahead) % 16], ring[place]) for place in range(16)]
        planes.append(lax.ppermute(gauge, ("z", "pb"), pairs))
    planes = jnp.stack(planes)
    products, number, target = call(
        right_kernel,
        [f32(4, 2, 2, W, LANES)] + [jax.ShapeDtypeStruct((1,), jnp.int32)] * 2,
        [VMEM, VMEM, SMEM],
        1 << 27,
        out_specs=[VMEM, SMEM, SMEM],
    )(in_hbm(coupling), in_hbm(gauge), kq_index.T)
    products = spread(products)
    branches = [functools.partial(translated, number=number) for number in range(16)]
    kept = lax.switch(number[0], branches, planes)
    swapped = lax.ppermute(kept, "core", [(0, 1), (1, 0)])
    high, low, *packs = call(
        owners_kernel,
        [jax.ShapeDtypeStruct((2 * NK, NK), jnp.bfloat16)] * 2 + [f32(264, LANES)] * 4,
        [VMEM] * 7,
        1 << 20,
    )(
        *(
            in_hbm(value)
            for value in (
                fine_coords,
                jnp.asarray(phase_tables()),
                eig_left,
                eig_right,
                energy_k,
                energy_kq,
                occupied,
            )
        )
    )
    pieces = call(left_kernel, f32(1024, LANES), [SMEM] + [VMEM] * 3, 1 << 27)(
        target, kept, swapped, products
    )
    columns = lax.all_to_all(pieces.reshape(32, 32, LANES), ("y", "x", "core"), 0, 0, tiled=True)
    packs = shifted(packs)
    fixed = pl.BlockSpec((2 * NK, NK), lambda i: (0, 0))
    fine = call(
        fourier_kernel,
        f32(32, 4, 8, LANES),
        [fixed, fixed, pl.BlockSpec((32, 16, LANES), lambda i: (0, i, 0))],
        1 << 28,
        grid=(2,),
        out_specs=pl.BlockSpec((32, 2, 8, LANES), lambda i: (0, i, 0, 0)),
    )(high, low, columns)
    blocks = lax.all_to_all(
        fine.reshape(32, 32, LANES), ("y", "x", "core"), 0, 0, tiled=True
    )
    terms = call(bloch_kernel, f32(16, 1, LANES), [SMEM] + [VMEM] * 5, 1 << 27)(
        frequency, blocks.reshape(1024, LANES), *packs
    )
    terms = lax.all_to_all(terms, ("z", "pb"), 0, 0, tiled=True)
    return call(sum_kernel, f32(2, W), [VMEM], 1 << 12)(terms)


def solution(mesh):
    split = Mesh(mesh.devices.reshape(4, 4, 4, 2, mesh.shape["pb"]), (*KA, "pb"))
    return jax.shard_map(
        shards,
        mesh=split,
        in_specs=(
            P(KA, "pb", None, None, None),
            P(KA, None, None),
            P(None, KA),
            P(),
            P(KA, None, None),
            P(KA, "pb", None, None),
            P(KA, None),
            P(KA, "pb", None),
            P(KA, "pb", None),
            P("pb", None),
        ),
        out_specs=P(KA, None),
        check_vma=False,
    )
```

```python
import functools
import math

import jax
import jax.numpy as jnp
import numpy as np
from jax import lax
from jax.experimental import pallas as pl
from jax.experimental.pallas import tpu as pltpu
from jax.sharding import Mesh
from jax.sharding import PartitionSpec as P

FG = 32
W = 64
LANES = 128
NK = 256
BROADEN = 0.1
THERMAL = 0.05
KA = ("z", "y", "x", "core")
VMEM = pl.BlockSpec(memory_space=pltpu.VMEM)
SMEM = pl.BlockSpec(memory_space=pltpu.SMEM)


def halves(value):
    high = value.astype(jnp.bfloat16)
    low = (value - high.astype(jnp.float32)).astype(jnp.bfloat16)
    return high, low


def product(left, right, axes):
    left_high, left_low = left
    right_high, right_low = right
    return lax.dot_general(
        jnp.concatenate([left_high, left_high, left_low], axes[0]),
        jnp.concatenate([right_high, right_low, right_high], axes[1]),
        (((axes[0],), (axes[1],)), ((), ())),
        preferred_element_type=jnp.float32,
    )


def right_block(matrix):
    turned = signs(-1.0) * pltpu.roll(matrix, W, 1)
    high, low = halves(matrix)
    turned_high, turned_low = halves(turned)
    return jnp.concatenate([high, turned_high], 0), jnp.concatenate([low, turned_low], 0)


def signs(first):
    lane = lax.broadcasted_iota(jnp.int32, (1, LANES), 1)
    return jnp.where(lane < W, first, -first)


def apply_left(left, right_pair):
    both = product(halves(left), halves(right_pair), (0, 0))
    sign = signs(1.0)
    return [
        both[:W, at : at + LANES] + sign * pltpu.roll(both[W:, at : at + LANES], W, 1)
        for at in (0, LANES)
    ]


def translation(number):
    along_second, along_first = number % 8, number // 8
    pairs = []
    for y in range(4):
        for x in range(4):
            second = ((y % 2) * 4 + x + along_second) % 8
            first = (y // 2 + along_first) % 2
            pairs.append(((first * 2 + second // 4) * 4 + second % 4, y * 4 + x))
    return pairs


def translated(value, number):
    pairs = translation(number)
    if all(source == target for source, target in pairs):
        return value
    return lax.ppermute(value, ("y", "x"), pairs)


def right_kernel(coupling, gauge, kq, out, number, target):
    along_z, along_y, along_x, pb = (lax.axis_index(name) for name in ("z", "y", "x", "pb"))
    point = kq[0, pb * 4 + along_z]
    target[0] = point
    number[0] = (((point >> 2) - (along_y * 4 + along_x)) & 7) + (
        (((point >> 5) - (along_y >> 1)) & 1) << 3
    )
    rows = coupling[0].reshape(-1, LANES)
    result = product(halves(rows), right_block(gauge[0]), (1, 0)).reshape(4, 2, W, LANES)
    out[:, 0] = result


def owners_kernel(
    coords, tables, eig_left, eig_right, energy_k, energy_kq, occupied, high, low, *outs
):
    pack_part(eig_left, eig_right, energy_k, energy_kq, occupied, outs)
    phase_part(coords, tables, high, low)


def pack_part(eig_left, eig_right, energy_k, energy_kq, occupied, outs):
    for shift, out in enumerate(outs):
        q = (lax.axis_index("z") + shift) & 3
        for f in range(2):
            out[f * W : f * W + W] = eig_left[f, q]
            out[LANES + f * W : LANES + f * W + W] = eig_right[f]
            filled = occupied[f, pl.ds(q, 1), :].astype(jnp.float32)
            row = 2 * LANES + f
            out[row : row + 1] = jnp.concatenate([energy_k[f : f + 1], energy_k[f : f + 1]], -1)
            out[row + 2 : row + 3] = jnp.concatenate([energy_kq[f, pl.ds(q, 1), :], filled], -1)
        out[2 * LANES + 4 :] = jnp.zeros((4, LANES), jnp.float32)


def left_kernel(target, kept, swapped, products, out):
    along_z, along_y, core = (lax.axis_index(name) for name in ("z", "y", "core"))
    target = target[0]
    first = (target >> 5) - 2 * along_z - (along_y >> 1)
    carry = ((along_y >> 1) + (first & 7)) >> 1
    wanniers = []
    for l in range(2):
        third = (target + l) & 3
        mine = (third >> 1) == core
        for z in range(4):
            plane = (z + carry - along_z + 4) & 3
            gauge = jnp.where(mine, kept[plane, third & 1], swapped[plane, third & 1])
            pair = jnp.concatenate([products[z, l, 0], products[z, l, 1]], -1)
            wanniers.append((l, z, apply_left(gauge, pair)))
    for l, z, both in wanniers:
        for b, wannier in enumerate(both):
            for part in range(2):
                start = (part * 2 + b) * 8 + z * 2 + l
                out[pl.ds(start, 32, stride=32), :] = wannier[part * 32 : part * 32 + 32]


def phase_part(coords, tables, high, low):
    source = lax.broadcasted_iota(jnp.int32, (NK, NK), 0)
    row = lax.broadcasted_iota(jnp.int32, (NK, NK), 1)
    wanted = (((row >> 1) & 3) << 6) + ((row >> 3) << 1) + (row & 1)
    turn = (source == wanted).astype(jnp.float32).astype(jnp.bfloat16)
    points = coords[...].astype(jnp.float32).astype(jnp.bfloat16)
    coords = jnp.dot(points, turn, preferred_element_type=jnp.float32)
    real, imag = None, None
    divisions = lax.broadcasted_iota(jnp.int32, (FG, NK), 0).astype(jnp.float32)
    for axis in range(3):
        onehot = (divisions == coords[axis : axis + 1, :]).astype(jnp.float32)
        onehot = onehot.astype(jnp.bfloat16)
        factor = lax.dot_general(
            jnp.concatenate([onehot] * 3, 0),
            tables[axis],
            (((0,), (0,)), ((), ())),
            preferred_element_type=jnp.float32,
        )
        factor = factor[:, :NK], factor[:, NK:]
        if real is None:
            real, imag = factor
        else:
            real, imag = (
                real * factor[0] - imag * factor[1],
                real * factor[1] + imag * factor[0],
            )
    for row, part in enumerate((real, imag)):
        part_high, part_low = halves(part)
        high[row * NK : row * NK + NK] = part_high
        low[row * NK : row * NK + NK] = part_low


def fourier_kernel(high, low, columns, out):
    parts = [columns[:, at : at + 8, :].reshape(NK, LANES) for at in (0, 8)]
    result = product((high[...], low[...]), halves(jnp.concatenate(parts, -1)), (1, 0))
    sign = signs(-1.0)
    for c in range(2):
        at = c * LANES
        rolled = pltpu.roll(result[NK:, at : at + LANES], W, 1)
        value = result[:NK, at : at + LANES] + sign * rolled
        out[:, c] = value.reshape(32, 8, LANES)


def bloch_kernel(frequency, arrived, *packs_and_out):
    packs, out = packs_and_out[:4], packs_and_out[4]
    lane = lax.broadcasted_iota(jnp.int32, (1, LANES), 1)
    first = lane < W
    phonons = [
        jnp.full((1, LANES), frequency[lax.axis_index("z"), b], jnp.float32) for b in range(2)
    ]
    boses = [1.0 / (jnp.exp(phonon / THERMAL) - 1.0) for phonon in phonons]
    scales = [1.0 / (2.0 * phonon) for phonon in phonons]
    pairs = []
    for shift, pack in enumerate(packs):
        plane = (lax.axis_index("z") - shift + 4) & 3
        for f in range(2):
            rows = [
                arrived[pl.ds((part * 2 + b) * 8 + plane * 2 + f, 32, stride=32), :]
                for b in range(2)
                for part in range(2)
            ]
            eig_right = pack[LANES + f * W : LANES + f * W + W]
            half = product(halves(jnp.concatenate(rows, 0)), right_block(eig_right), (1, 0))
            pairs.append(jnp.concatenate([half[:W], half[W:]], -1))
    squares = []
    for shift, pack in enumerate(packs):
        for f in range(2):
            blochs = apply_left(pack[f * W : f * W + W], pairs[shift * 2 + f])
            squares.append([bloch * bloch for bloch in blochs])
    for shift, pack in enumerate(packs):
        tail = pack[2 * LANES :]
        energies = jnp.where(first, tail[0:1], tail[1:2])
        states = tail.T
        energy_left = jnp.where(first, states[:W, 2:3], states[:W, 3:4])
        filled = jnp.where(first, states[W:, 2:3], states[W:, 3:4])
        gap = energies - energy_left
        total = jnp.zeros((W, LANES), jnp.float32)
        for b, (phonon, bose) in enumerate(zip(phonons, boses)):
            up = gap + phonon
            down = gap - phonon
            up_square = up * up + BROADEN * BROADEN
            down_square = down * down + BROADEN * BROADEN
            terms = (bose + filled) * up * down_square + (bose + 1.0 - filled) * down * up_square
            one, two = squares[shift * 2][b], squares[shift * 2 + 1][b]
            strength = jnp.where(first, one, two) + pltpu.roll(jnp.where(first, two, one), W, 1)
            total = total + strength * scales[b] * terms / (up_square * down_square)
        summed = jnp.sum(total, axis=0, keepdims=True) * (1.0 / 1024.0)
        plane = (lax.axis_index("z") - shift + 4) & 3
        for group in range(4):
            out[group * 4 + plane] = summed


def sum_kernel(terms, out):
    summed = jnp.sum(terms[...], axis=0)
    out[0:1] = summed[:, :W]
    out[1:2] = summed[:, W:]


def phase_tables():
    column = np.arange(NK)
    source, z, l = column // 8, column // 2 % 4, column % 2
    y, x, core = source // 8, source // 2 % 4, source % 2
    coordinates = (2 * z + y // 2, (y % 2) * 4 + x, 2 * core + l)
    tables = np.zeros((3, 2, FG, NK), np.float64)
    for axis, (size, where) in enumerate(zip((8, 8, 4), coordinates)):
        steps = np.arange(FG)[:, None] - (FG // size) * where[None, :]
        for cell in range(-size // 2, size // 2):
            angle = 2.0 * math.pi * ((cell * steps) % FG) / FG
            tables[axis, 0] += np.cos(angle) / size
            tables[axis, 1] += np.sin(angle) / size
    tables = np.concatenate([tables[:, 0], tables[:, 1]], -1)
    terms = []
    for _ in range(3):
        terms.append(tables.astype(jnp.bfloat16))
        tables = tables - terms[-1].astype(np.float64)
    return np.concatenate(terms, 1)


def call(kernel, shapes, specs, flops, vmem=16, **more):
    return pl.pallas_call(
        kernel,
        out_shape=shapes,
        in_specs=specs,
        cost_estimate=pl.CostEstimate(flops=flops, bytes_accessed=1 << 20, transcendentals=0),
        compiler_params=pltpu.CompilerParams(vmem_limit_bytes=vmem << 20),
        **more,
    )


def f32(*shape):
    return jax.ShapeDtypeStruct(shape, jnp.float32)


def spread(value):
    return lax.all_to_all(value, "z", 0, 0, tiled=True)


def in_hbm(value):
    return pltpu.with_memory_space_constraint(value, pltpu.HBM)


def shifted(values):
    arrived = [values[0]]
    for shift in (1, 2, 3):
        pairs = [(z, (z + shift) % 4) for z in range(4)]
        arrived.append(lax.ppermute(values[shift], "z", pairs))
    return arrived


def shards(
    coupling,
    gauge,
    kq_index,
    fine_coords,
    eig_right,
    eig_left,
    energy_k,
    energy_kq,
    occupied,
    frequency,
):
    along_z, along_y, along_x, core = (lax.axis_index(name) for name in KA)
    planes = [gauge]
    for ahead in (1, 2, 15):
        ring = [place % 4 * 4 + place // 4 for place in range(16)]
        pairs = [(ring[(place + ahead) % 16], ring[place]) for place in range(16)]
        planes.append(lax.ppermute(gauge, ("z", "pb"), pairs))
    planes = jnp.stack(planes)
    products, number, target = call(
        right_kernel,
        [f32(4, 2, 2, W, LANES)] + [jax.ShapeDtypeStruct((1,), jnp.int32)] * 2,
        [
            pl.BlockSpec((1, 4, 2, W, LANES), lambda k: (k, 0, 0, 0, 0)),
            pl.BlockSpec((1, W, LANES), lambda k: (k, 0, 0)),
            SMEM,
        ],
        1 << 27,
        grid=(2,),
        out_specs=[
            pl.BlockSpec((4, 1, 2, W, LANES), lambda k: (0, k, 0, 0, 0)),
            SMEM,
            SMEM,
        ],
    )(in_hbm(coupling), in_hbm(gauge), kq_index.T)
    products = spread(products)
    branches = [functools.partial(translated, number=number) for number in range(16)]
    kept = lax.switch(number[0], branches, planes)
    swapped = lax.ppermute(kept, "core", [(0, 1), (1, 0)])
    high, low, *packs = call(
        owners_kernel,
        [jax.ShapeDtypeStruct((2 * NK, NK), jnp.bfloat16)] * 2 + [f32(264, LANES)] * 4,
        [VMEM] * 7,
        1 << 20,
    )(
        *(
            in_hbm(value)
            for value in (
                fine_coords,
                jnp.asarray(phase_tables()),
                eig_left,
                eig_right,
                energy_k,
                energy_kq,
                occupied,
            )
        )
    )
    pieces = call(left_kernel, f32(1024, LANES), [SMEM] + [VMEM] * 3, 1 << 27)(
        target, kept, swapped, products
    )
    columns = lax.all_to_all(pieces.reshape(32, 32, LANES), ("y", "x", "core"), 0, 0, tiled=True)
    packs = shifted(packs)
    fixed = pl.BlockSpec((2 * NK, NK), lambda i: (0, 0))
    fine = call(
        fourier_kernel,
        f32(32, 4, 8, LANES),
        [fixed, fixed, pl.BlockSpec((32, 16, LANES), lambda i: (0, i, 0))],
        1 << 28,
        grid=(2,),
        out_specs=pl.BlockSpec((32, 2, 8, LANES), lambda i: (0, i, 0, 0)),
    )(high, low, columns)
    blocks = lax.all_to_all(
        fine.reshape(32, 32, LANES), ("y", "x", "core"), 0, 0, tiled=True
    )
    terms = call(bloch_kernel, f32(16, 1, LANES), [SMEM] + [VMEM] * 5, 1 << 27)(
        frequency, blocks.reshape(1024, LANES), *packs
    )
    terms = lax.all_to_all(terms, ("pb", "z"), 0, 0, tiled=True)
    return call(sum_kernel, f32(2, W), [VMEM], 1 << 12)(terms)


def solution(mesh):
    split = Mesh(mesh.devices.reshape(4, 4, 4, 2, mesh.shape["pb"]), (*KA, "pb"))
    return jax.shard_map(
        shards,
        mesh=split,
        in_specs=(
            P(KA, "pb", None, None, None),
            P(KA, None, None),
            P(None, KA),
            P(),
            P(KA, None, None),
            P(KA, "pb", None, None),
            P(KA, None),
            P(KA, "pb", None),
            P(KA, "pb", None),
            P("pb", None),
        ),
        out_specs=P(KA, None),
        check_vma=False,
    )
```

```python
import functools
import math

import jax
import jax.numpy as jnp
import numpy as np
from jax import lax
from jax.experimental import pallas as pl
from jax.experimental.pallas import tpu as pltpu
from jax.sharding import Mesh
from jax.sharding import PartitionSpec as P

FG = 32
W = 64
LANES = 128
NK = 256
BROADEN = 0.1
THERMAL = 0.05
KA = ("z", "y", "x", "core")
VMEM = pl.BlockSpec(memory_space=pltpu.VMEM)
SMEM = pl.BlockSpec(memory_space=pltpu.SMEM)


def halves(value):
    high = value.astype(jnp.bfloat16)
    low = (value - high.astype(jnp.float32)).astype(jnp.bfloat16)
    return high, low


def product(left, right, axes):
    left_high, left_low = left
    right_high, right_low = right
    return lax.dot_general(
        jnp.concatenate([left_high, left_high, left_low], axes[0]),
        jnp.concatenate([right_high, right_low, right_high], axes[1]),
        (((axes[0],), (axes[1],)), ((), ())),
        preferred_element_type=jnp.float32,
    )


def right_block(matrix):
    turned = signs(-1.0) * pltpu.roll(matrix, W, 1)
    high, low = halves(matrix)
    turned_high, turned_low = halves(turned)
    return jnp.concatenate([high, turned_high], 0), jnp.concatenate([low, turned_low], 0)


def signs(first):
    lane = lax.broadcasted_iota(jnp.int32, (1, LANES), 1)
    return jnp.where(lane < W, first, -first)


def apply_left(left, right_pair):
    both = product(halves(left), halves(right_pair), (0, 0))
    sign = signs(1.0)
    return [
        both[:W, at : at + LANES] + sign * pltpu.roll(both[W:, at : at + LANES], W, 1)
        for at in (0, LANES)
    ]


def translation(number):
    along_second, along_first = number % 8, number // 8
    pairs = []
    for y in range(4):
        for x in range(4):
            second = ((y % 2) * 4 + x + along_second) % 8
            first = (y // 2 + along_first) % 2
            pairs.append(((first * 2 + second // 4) * 4 + second % 4, y * 4 + x))
    return pairs


def translated(value, number):
    pairs = translation(number)
    if all(source == target for source, target in pairs):
        return value
    return lax.ppermute(value, ("y", "x"), pairs)


def right_kernel(coupling, gauge, kq, out, number, target):
    along_z, along_y, along_x, pb = (lax.axis_index(name) for name in ("z", "y", "x", "pb"))
    point = kq[0, pb * 4 + along_z]
    target[0] = point
    number[0] = (((point >> 2) - (along_y * 4 + along_x)) & 7) + (
        (((point >> 5) - (along_y >> 1)) & 1) << 3
    )
    for k in range(2):
        rows = coupling[k].reshape(-1, LANES)
        result = product(halves(rows), right_block(gauge[k]), (1, 0)).reshape(4, 2, W, LANES)
        for q in range(4):
            out[q, k] = result[q]


def owners_kernel(
    coords, tables, eig_left, eig_right, energy_k, energy_kq, occupied, high, low, *outs
):
    pack_part(eig_left, eig_right, energy_k, energy_kq, occupied, outs)
    phase_part(coords, tables, high, low)


def pack_part(eig_left, eig_right, energy_k, energy_kq, occupied, outs):
    for shift, out in enumerate(outs):
        q = (lax.axis_index("z") + shift) & 3
        for f in range(2):
            out[f * W : f * W + W] = eig_left[f, q]
            out[LANES + f * W : LANES + f * W + W] = eig_right[f]
            filled = occupied[f, pl.ds(q, 1), :].astype(jnp.float32)
            row = 2 * LANES + f
            out[row : row + 1] = jnp.concatenate([energy_k[f : f + 1], energy_k[f : f + 1]], -1)
            out[row + 2 : row + 3] = jnp.concatenate([energy_kq[f, pl.ds(q, 1), :], filled], -1)
        out[2 * LANES + 4 :] = jnp.zeros((4, LANES), jnp.float32)


def left_kernel(target, kept, swapped, products, out):
    along_z, along_y, core = (lax.axis_index(name) for name in ("z", "y", "core"))
    target = target[0]
    first = (target >> 5) - 2 * along_z - (along_y >> 1)
    carry = ((along_y >> 1) + (first & 7)) >> 1
    wanniers = []
    for l in range(2):
        third = (target + l) & 3
        mine = (third >> 1) == core
        for z in range(4):
            plane = (z + carry - along_z + 4) & 3
            gauge = jnp.where(mine, kept[plane, third & 1], swapped[plane, third & 1])
            pair = jnp.concatenate([products[z, l, 0], products[z, l, 1]], -1)
            wanniers.append((l, z, apply_left(gauge, pair)))
    for l, z, both in wanniers:
        for b, wannier in enumerate(both):
            for part in range(2):
                start = (part * 2 + b) * 8 + z * 2 + l
                out[pl.ds(start, 32, stride=32), :] = wannier[part * 32 : part * 32 + 32]


def phase_part(coords, tables, high, low):
    source = lax.broadcasted_iota(jnp.int32, (NK, NK), 0)
    row = lax.broadcasted_iota(jnp.int32, (NK, NK), 1)
    wanted = (((row >> 1) & 3) << 6) + ((row >> 3) << 1) + (row & 1)
    turn = (source == wanted).astype(jnp.float32).astype(jnp.bfloat16)
    points = coords[...].astype(jnp.float32).astype(jnp.bfloat16)
    coords = jnp.dot(points, turn, preferred_element_type=jnp.float32)
    real, imag = None, None
    divisions = lax.broadcasted_iota(jnp.int32, (FG, NK), 0).astype(jnp.float32)
    for axis in range(3):
        onehot = (divisions == coords[axis : axis + 1, :]).astype(jnp.float32)
        onehot = onehot.astype(jnp.bfloat16)
        factor = lax.dot_general(
            jnp.concatenate([onehot] * 3, 0),
            tables[axis],
            (((0,), (0,)), ((), ())),
            preferred_element_type=jnp.float32,
        )
        factor = factor[:, :NK], factor[:, NK:]
        if real is None:
            real, imag = factor
        else:
            real, imag = (
                real * factor[0] - imag * factor[1],
                real * factor[1] + imag * factor[0],
            )
    for row, part in enumerate((real, imag)):
        part_high, part_low = halves(part)
        high[row * NK : row * NK + NK] = part_high
        low[row * NK : row * NK + NK] = part_low


def fourier_kernel(high, low, columns, out):
    parts = [columns[:, at : at + 8, :].reshape(NK, LANES) for at in (0, 8)]
    result = product((high[...], low[...]), halves(jnp.concatenate(parts, -1)), (1, 0))
    sign = signs(-1.0)
    for c in range(2):
        at = c * LANES
        rolled = pltpu.roll(result[NK:, at : at + LANES], W, 1)
        value = result[:NK, at : at + LANES] + sign * rolled
        out[:, c] = value.reshape(32, 8, LANES)


def bloch_kernel(frequency, arrived, *packs_and_out):
    packs, out = packs_and_out[:4], packs_and_out[4]
    lane = lax.broadcasted_iota(jnp.int32, (1, LANES), 1)
    first = lane < W
    phonons = [
        jnp.full((1, LANES), frequency[lax.axis_index("z"), b], jnp.float32) for b in range(2)
    ]
    boses = [1.0 / (jnp.exp(phonon / THERMAL) - 1.0) for phonon in phonons]
    scales = [1.0 / (2.0 * phonon) for phonon in phonons]
    pairs = []
    for shift, pack in enumerate(packs):
        plane = (lax.axis_index("z") - shift + 4) & 3
        for f in range(2):
            rows = [
                arrived[pl.ds((part * 2 + b) * 8 + plane * 2 + f, 32, stride=32), :]
                for b in range(2)
                for part in range(2)
            ]
            eig_right = pack[LANES + f * W : LANES + f * W + W]
            half = product(halves(jnp.concatenate(rows, 0)), right_block(eig_right), (1, 0))
            pairs.append(jnp.concatenate([half[:W], half[W:]], -1))
    squares = []
    for shift, pack in enumerate(packs):
        for f in range(2):
            blochs = apply_left(pack[f * W : f * W + W], pairs[shift * 2 + f])
            squares.append([bloch * bloch for bloch in blochs])
    for shift, pack in enumerate(packs):
        tail = pack[2 * LANES :]
        energies = jnp.where(first, tail[0:1], tail[1:2])
        states = tail.T
        energy_left = jnp.where(first, states[:W, 2:3], states[:W, 3:4])
        filled = jnp.where(first, states[W:, 2:3], states[W:, 3:4])
        gap = energies - energy_left
        total = jnp.zeros((W, LANES), jnp.float32)
        for b, (phonon, bose) in enumerate(zip(phonons, boses)):
            up = gap + phonon
            down = gap - phonon
            up_square = up * up + BROADEN * BROADEN
            down_square = down * down + BROADEN * BROADEN
            terms = (bose + filled) * up * down_square + (bose + 1.0 - filled) * down * up_square
            one, two = squares[shift * 2][b], squares[shift * 2 + 1][b]
            strength = jnp.where(first, one, two) + pltpu.roll(jnp.where(first, two, one), W, 1)
            total = total + strength * scales[b] * terms / (up_square * down_square)
        summed = jnp.sum(total, axis=0, keepdims=True) * (1.0 / 1024.0)
        plane = (lax.axis_index("z") - shift + 4) & 3
        for group in range(4):
            out[plane * 4 + group] = summed


def sum_kernel(terms, out):
    summed = jnp.sum(terms[...], axis=0)
    out[0:1] = summed[:, :W]
    out[1:2] = summed[:, W:]


def phase_tables():
    column = np.arange(NK)
    source, z, l = column // 8, column // 2 % 4, column % 2
    y, x, core = source // 8, source // 2 % 4, source % 2
    coordinates = (2 * z + y // 2, (y % 2) * 4 + x, 2 * core + l)
    tables = np.zeros((3, 2, FG, NK), np.float64)
    for axis, (size, where) in enumerate(zip((8, 8, 4), coordinates)):
        steps = np.arange(FG)[:, None] - (FG // size) * where[None, :]
        for cell in range(-size // 2, size // 2):
            angle = 2.0 * math.pi * ((cell * steps) % FG) / FG
            tables[axis, 0] += np.cos(angle) / size
            tables[axis, 1] += np.sin(angle) / size
    tables = np.concatenate([tables[:, 0], tables[:, 1]], -1)
    terms = []
    for _ in range(3):
        terms.append(tables.astype(jnp.bfloat16))
        tables = tables - terms[-1].astype(np.float64)
    return np.concatenate(terms, 1)


def call(kernel, shapes, specs, flops, vmem=16, **more):
    return pl.pallas_call(
        kernel,
        out_shape=shapes,
        in_specs=specs,
        cost_estimate=pl.CostEstimate(flops=flops, bytes_accessed=1 << 20, transcendentals=0),
        compiler_params=pltpu.CompilerParams(vmem_limit_bytes=vmem << 20),
        **more,
    )


def f32(*shape):
    return jax.ShapeDtypeStruct(shape, jnp.float32)


def spread(value):
    return lax.all_to_all(value, "z", 0, 0, tiled=True)


def from_ring(value, ahead):
    ring = [place % 4 * 4 + place // 4 for place in range(16)]
    pairs = [(ring[(place + ahead) % 16], ring[place]) for place in range(16)]
    return lax.ppermute(value, ("z", "pb"), pairs)


def in_hbm(value):
    return pltpu.with_memory_space_constraint(value, pltpu.HBM)


def shifted(values):
    arrived = [values[0]]
    for shift in (1, 2, 3):
        pairs = [(z, (z + shift) % 4) for z in range(4)]
        arrived.append(lax.ppermute(values[shift], "z", pairs))
    return arrived


def shards(
    coupling,
    gauge,
    kq_index,
    fine_coords,
    eig_right,
    eig_left,
    energy_k,
    energy_kq,
    occupied,
    frequency,
):
    along_z, along_y, along_x, core = (lax.axis_index(name) for name in KA)
    after = from_ring(gauge, 1)
    before = from_ring(gauge, 15)
    planes = [gauge, after, from_ring(after, 1), before]
    planes = jnp.stack(planes)
    products, number, target = call(
        right_kernel,
        [f32(4, 2, 2, W, LANES)] + [jax.ShapeDtypeStruct((1,), jnp.int32)] * 2,
        [VMEM, VMEM, SMEM],
        1 << 27,
        out_specs=[VMEM, SMEM, SMEM],
    )(in_hbm(coupling), in_hbm(gauge), kq_index.T)
    products = spread(products)
    branches = [functools.partial(translated, number=number) for number in range(16)]
    kept = lax.switch(number[0], branches, planes)
    swapped = lax.ppermute(kept, "core", [(0, 1), (1, 0)])
    high, low, *packs = call(
        owners_kernel,
        [jax.ShapeDtypeStruct((2 * NK, NK), jnp.bfloat16)] * 2 + [f32(264, LANES)] * 4,
        [VMEM] * 7,
        1 << 20,
    )(
        *(
            in_hbm(value)
            for value in (
                fine_coords,
                jnp.asarray(phase_tables()),
                eig_left,
                eig_right,
                energy_k,
                energy_kq,
                occupied,
            )
        )
    )
    pieces = call(left_kernel, f32(1024, LANES), [SMEM] + [VMEM] * 3, 1 << 27)(
        target, kept, swapped, products
    )
    columns = lax.all_to_all(pieces.reshape(32, 32, LANES), ("y", "x", "core"), 0, 0, tiled=True)
    packs = shifted(packs)
    fixed = pl.BlockSpec((2 * NK, NK), lambda i: (0, 0))
    fine = call(
        fourier_kernel,
        f32(32, 4, 8, LANES),
        [fixed, fixed, pl.BlockSpec((32, 16, LANES), lambda i: (0, i, 0))],
        1 << 28,
        grid=(2,),
        out_specs=pl.BlockSpec((32, 2, 8, LANES), lambda i: (0, i, 0, 0)),
    )(high, low, columns)
    blocks = lax.all_to_all(
        fine.reshape(32, 32, LANES), ("y", "x", "core"), 0, 0, tiled=True
    )
    terms = call(bloch_kernel, f32(16, 1, LANES), [SMEM] + [VMEM] * 5, 1 << 27)(
        frequency, blocks.reshape(1024, LANES), *packs
    )
    terms = lax.all_to_all(terms, ("z", "pb"), 0, 0, tiled=True)
    return call(sum_kernel, f32(2, W), [VMEM], 1 << 12)(terms)


def solution(mesh):
    split = Mesh(mesh.devices.reshape(4, 4, 4, 2, mesh.shape["pb"]), (*KA, "pb"))
    return jax.shard_map(
        shards,
        mesh=split,
        in_specs=(
            P(KA, "pb", None, None, None),
            P(KA, None, None),
            P(None, KA),
            P(),
            P(KA, None, None),
            P(KA, "pb", None, None),
            P(KA, None),
            P(KA, "pb", None),
            P(KA, "pb", None),
            P("pb", None),
        ),
        out_specs=P(KA, None),
        check_vma=False,
    )
```
